32 devices in a mesh: sub: 4 (over x, core), tile: 8 (over z, y).
Axes of the slice: x: 2, y: 2, z: 4, core: 2. Of those that a mesh axis runs over, the one named last changes fastest.
Arguments:
- states: float32 [4, 3, 256, 2048], P('sub', None, 'tile'), may hold values from -6 to 6
- terrain: int32 [256, 2048], P('tile'), may hold values from 0 to 7
- depth_table: float32 [8], replicated, may hold values from 0.5 to 2
- spread_table: float32 [8], replicated, may hold values from 0.03 to 0.24
- mixing: float32 [4, 4], replicated, may hold values from -0.9 to 2, as said below
Outputs:
- gradient: float32 [4, 3, 256, 2048], P('sub', None, 'tile')
The draws below stay inside these ranges and needn't reach their ends.
Inputs may be any that keep to these rules, and one draw needn't show every extreme that they name: `mixing`: A dense matrix with diagonal entries between 1 and 2.
All inputs are finite; a program needn't handle non-finite values.
Results may differ from the reference program's by a relative error of at most 0.00012.
Values sent between devices are 32-bit elements; how exact they have to be, the bound alone decides.
A program may use at most 64 MiB of HBM per device.

```python
import math
import jax
import jax.numpy as jnp
from jax import lax

NY = 2048
NCLASS = 8
FSTEPS = 3
DSTEPS = 3
S = 4
NX = 256


def draw_mixing(key, part):
    first_key = jax.random.fold_in(key, 11)
    second_key = jax.random.fold_in(key, 12)
    diagonal = jax.random.uniform(first_key, (S,), jnp.float32, 1.0, 2.0)
    off = jnp.clip(0.3 * jax.random.normal(second_key, (S, S), jnp.float32), -0.9, 0.9)
    eye = jnp.eye(S, dtype=jnp.float32)
    return off * (1.0 - eye) + eye * diagonal[None, :]


def touch_ends(entries, stream_key, smallest, largest):
    longest = entries.shape.index(max(entries.shape))
    spots = []
    for shift in (0, 1):
        where = [jax.random.randint(jax.random.fold_in(stream_key, axis), (), 0, length) for axis, length in enumerate(entries.shape)]
        where[longest] = (where[longest] + shift) % entries.shape[longest]
        spots.append(tuple(where))
    return entries.at[spots[0]].set(smallest).at[spots[1]].set(largest)


def steps_of(rng, extent, cuts, smallest, largest):
    def one(position, blocks):
        heights = jax.random.uniform(jax.random.fold_in(jax.random.fold_in(rng, 6), position), (blocks,), jnp.float32, smallest / len(cuts), largest / len(cuts))
        return jnp.repeat(jnp.exp(heights), extent[position] // blocks).reshape((-1,) + (1,) * (len(extent) - position - 1))

    gain = one(*cuts[0])
    for cut in cuts[1:]:
        gain = gain * one(*cut)
    return gain


def scatter_about(rng, shape, width, bound, shards=(), kind=jnp.bfloat16):
    entries = jax.random.normal(rng, shape, jnp.float32) * width
    if len(shards) > 0:
        entries = steps_of(rng, shape, shards, -0.22, 0.18) * entries
    return jnp.clip(entries, min=-bound, max=bound).astype(kind)


def setup_inputs(seed: int = 0) -> dict:
    keys = jax.random.split(jax.random.key(seed), 6)
    return {
        "states": scatter_about(keys[0], (S, 3, NX, NY), 1.0, 6.0, ((0, 4), (2, 8)), jnp.float32),
        "terrain": touch_ends(jax.random.randint(keys[1], (NX, NY), 0, NCLASS), jax.random.fold_in(keys[1], 1), 0, NCLASS - 1).astype(jnp.int32),
        "depth_table": jnp.clip(jnp.exp(jax.random.uniform(keys[2], (NCLASS,), jnp.float32, math.log(0.5), math.log(2.0))), 0.5, 2.0),
        "spread_table": jnp.clip(jax.random.uniform(keys[3], (NCLASS,), jnp.float32, 0.03, 0.24), 0.03, 0.24),
        "mixing": draw_mixing(jax.random.fold_in(keys[5], 71), 0),
    }


time_step = 0.5
gravity = 1.0
coriolis = 0.3


def col_diff(field):
    return (jnp.roll(field, -1, -1) - jnp.roll(field, 1, -1)) * 0.5


def row_mask(first, count, total):
    index = first + jnp.arange(count, dtype=jnp.int32)
    return ((index >= 0) & (index < total)).astype(jnp.float32)[:, None]


def model_step(state, depth, first, total):
    height, east, north = state[0], state[1], state[2]
    flux_x = depth * east
    flux_y = depth * north
    new_h = height[1:-1] - time_step * ((flux_x[2:] - flux_x[:-2]) * 0.5 + col_diff(flux_y[1:-1]))
    new_h = new_h * row_mask(first + 1, new_h.shape[0], total)
    new_u = east[2:-2] - time_step * gravity * (new_h[2:] - new_h[:-2]) * 0.5 + time_step * coriolis * north[2:-2]
    new_v = north[2:-2] - time_step * gravity * col_diff(new_h[1:-1]) - time_step * coriolis * east[2:-2]
    result = jnp.stack([new_h[1:-1], new_u, new_v])
    return result * row_mask(first + 2, result.shape[1], total)


def spread_step(field, kappa, first, total):
    centre = field[:, 1:-1]
    laplace = field[:, 2:] + field[:, :-2] + jnp.roll(centre, 1, 2) + jnp.roll(centre, -1, 2) - 4.0 * centre
    return (centre + kappa * laplace) * row_mask(first + 1, centre.shape[1], total)


def reference(states, terrain, depth_table, spread_table, mixing):
    classes = jnp.arange(NCLASS, dtype=jnp.int32)
    pick = (terrain[None] == classes[:, None, None]).astype(jnp.float32)
    depth = jnp.sum(pick * depth_table[:, None, None], 0)
    kappa = jnp.sum(pick * spread_table[:, None, None], 0)
    depth_pad = jnp.pad(depth, ((2, 2), (0, 0)))

    def forward(state):
        for step in range(FSTEPS):
            padded = jnp.pad(state, ((0, 0), (2, 2), (0, 0)))
            state = model_step(padded, depth_pad, -2, NX)
        return state

    ends = lax.map(forward, states)
    earlier = jnp.concatenate([jnp.zeros_like(ends[:1]), ends[:-1]], 0)
    jumps = states - earlier
    mixed = jnp.einsum("st,tfxy->sfxy", mixing, jumps, precision=lax.Precision.HIGHEST)

    def smooth(field):
        for step in range(DSTEPS):
            padded = jnp.pad(field, ((0, 0), (1, 1), (0, 0)))
            field = spread_step(padded, kappa, -1, NX)
        return field

    return lax.map(smooth, mixed)
```

```python
import functools

import jax
import jax.numpy as jnp
from jax import lax
from jax.experimental import pallas as pl
from jax.experimental.pallas import tpu as pltpu
from jax.sharding import PartitionSpec as P

FSTEPS = 3
DSTEPS = 3
time_step = 0.5
gravity = 1.0
coriolis = 0.3

LANES = 128
SUBLANES = 8
HALO = 2 * FSTEPS + DSTEPS
STEP = 3
DEPTH, KAPPA = 3, 4


def windows_of(rows):
    middle = rows // 2
    found = [(HALO, middle), (HALO, rows - HALO)]
    for reach in range(STEP, HALO + 1, STEP):
        found.append((HALO - reach, rows - HALO + reach))
    return found


def pieces_of(rows):
    last, place, pieces = None, 0, []
    for window in windows_of(rows):
        spans = [window] if last is None else [(window[0], last[0]), (last[1], window[1])]
        last = window
        held = []
        for lo, hi in spans:
            if hi > lo:
                held.append((lo, hi - lo, place))
                place += hi - lo
        pieces.append(held)
    return pieces


def kernel(
    subs, tiles, rows, cols, nclass,
    depth_in, spread_in, mixing_in, states, terrain, out,
    depth_tab, spread_tab, mixing, T, S, E, W, send_a, recv_a, send_b, recv_b, M,
    load_sem, land_send, land_recv, pass_send, pass_recv, halo_send, halo_recv, a_send, a_recv, b_send, b_recv,
):
    pairs = subs // 2
    blocks = cols // LANES
    half = blocks // 2
    me = lax.axis_index("sub")
    tile = lax.axis_index("tile")
    parity = lax.rem(me, 2)
    mate = me + 1 - 2 * parity
    pair = me // 2
    has_up = tile > 0
    has_down = tile < tiles - 1
    up, down = tile - 1, tile + 1
    windows, pieces = windows_of(rows), pieces_of(rows)
    groups = HALO // STEP

    tables = [
        pltpu.make_async_copy(depth_in, depth_tab, load_sem.at[2]),
        pltpu.make_async_copy(spread_in, spread_tab, load_sem.at[3]),
        pltpu.make_async_copy(mixing_in, mixing, load_sem.at[4]),
    ]
    for copy in tables:
        copy.start()

    own = pl.ds(HALO, rows)
    for b in range(blocks):
        at = pl.ds(b * LANES, LANES)
        pltpu.make_async_copy(terrain.at[:, at], T.at[:, b % 2, b // 2], load_sem.at[0]).start()
    for b in range(blocks):
        at = pl.ds(b * LANES, LANES)
        pltpu.make_async_copy(
            states.at[0, :, :, at], S.at[pl.ds(0, 3), own, b % 2, b // 2], load_sem.at[1]
        ).start()

    barrier = pltpu.get_barrier_semaphore()
    pl.semaphore_signal(barrier, inc=1, device_id={"sub": mate})
    for k in range(1, pairs):
        pl.semaphore_signal(
            barrier, inc=1, device_id={"sub": lax.rem(pair + k, pairs) * 2 + parity}
        )

    @pl.when(has_up)
    def _():
        pl.semaphore_signal(barrier, inc=1, device_id={"tile": up})

    @pl.when(has_down)
    def _():
        pl.semaphore_signal(barrier, inc=1, device_id={"tile": down})

    @pl.when(jnp.logical_not(has_up))
    def _():
        S[:, 0:HALO] = jnp.zeros((5, HALO, 2, half, LANES), jnp.float32)

    @pl.when(jnp.logical_not(has_down))
    def _():
        S[:, HALO + rows:] = jnp.zeros((5, HALO, 2, half, LANES), jnp.float32)

    pltpu.make_async_copy(T, T, load_sem.at[0]).wait()
    for copy in tables:
        copy.wait()
    batch = 8 if rows % 8 == 0 else 1

    def lookup(i, carry):
        kind = T[pl.ds(i * batch, batch)]
        depth = jnp.zeros(kind.shape, jnp.float32)
        kappa = jnp.zeros(kind.shape, jnp.float32)
        for n in range(nclass):
            hit = kind == n
            depth = jnp.where(hit, depth_tab[n], depth)
            kappa = jnp.where(hit, spread_tab[n], kappa)
        S[DEPTH, pl.ds(HALO + i * batch, batch)] = depth
        S[KAPPA, pl.ds(HALO + i * batch, batch)] = kappa
        return carry

    lax.fori_loop(0, rows // batch, lookup, 0)
    loaded = S.at[pl.ds(0, 3), own]
    pltpu.make_async_copy(loaded, loaded, load_sem.at[1]).wait()

    def edge(way, near, far):
        count = far - near + 1
        if way == 0:
            return pl.ds(HALO + rows - far, count), pl.ds(HALO - far, count)
        return pl.ds(HALO + near - 1, count), pl.ds(HALO + rows + near - 1, count)

    def to_tile(way, source, target, send, recv):
        return pltpu.make_async_remote_copy(
            src_ref=source, dst_ref=target, send_sem=send, recv_sem=recv,
            device_id={"tile": down if way == 0 else up}, device_id_type=pl.DeviceIdType.MESH,
        )

    land_rows = ((DEPTH, HALO), (KAPPA, DSTEPS - 1))
    land_bytes = S.at[0, pl.ds(0, HALO + DSTEPS - 1), 0]

    def land_copies(way):
        copies = []
        for f, far in land_rows:
            source, target = edge(way, 1, far)
            copies.append(to_tile(
                way, S.at[f, source, parity], S.at[f, target, parity],
                land_send.at[way], land_recv.at[way],
            ))
        return copies

    def pass_copies(way):
        copies = []
        for f, far in land_rows:
            _, at = edge(way, 1, far)
            copies.append(pltpu.make_async_remote_copy(
                src_ref=S.at[f, at, parity], dst_ref=S.at[f, at, parity],
                send_sem=pass_send.at[way], recv_sem=pass_recv.at[way],
                device_id={"sub": mate}, device_id_type=pl.DeviceIdType.MESH,
            ))
        return copies

    def halo_copies(way, g):
        near, far = g * STEP + 1, (g + 1) * STEP
        parts = [(pl.ds(0, 3), near, far)]
        if g == groups - 1:
            parts = [(pl.ds(0, 3), near, far - 1), (pl.ds(1, 1), far, far)]
        copies = []
        for fields, first, last in parts:
            source, target = edge(way, first, last)
            copies.append(to_tile(
                way, S.at[fields, source], S.at[fields, target],
                halo_send.at[way], halo_recv.at[way, g],
            ))
        return copies

    def halo_bytes(g):
        return S.at[0, pl.ds(0, 3 * STEP - (2 if g == groups - 1 else 0))]

    def wait_for(some, sem):
        pltpu.make_async_copy(some, some, sem).wait()

    comes = (has_up, has_down)
    goes = (has_down, has_up)

    def enter():
        pl.semaphore_wait(
            barrier, pairs + has_up.astype(jnp.int32) + has_down.astype(jnp.int32)
        )
        for way in range(2):

            @pl.when(goes[way])
            def _():
                for copy in land_copies(way):
                    copy.start()

        for way in range(2):

            @pl.when(goes[way])
            def _():
                for g in range(groups):
                    for copy in halo_copies(way, g):
                        copy.start()

    def pass_land():
        for way in range(2):

            @pl.when(comes[way])
            def _():
                wait_for(land_bytes, land_recv.at[way])
                for copy in pass_copies(way):
                    copy.start()

    def take_land():
        for way in range(2):

            @pl.when(comes[way])
            def _():
                wait_for(land_bytes, pass_recv.at[way])

    def take_halo(g):
        for way in range(2):

            @pl.when(comes[way])
            def _():
                wait_for(halo_bytes(g), halo_recv.at[way, g])

    lane = lax.broadcasted_iota(jnp.int32, (1, half, LANES), 2)
    is_first, is_last = lane == 0, lane == LANES - 1

    def get(ref, lead, start, count):
        at = pl.ds(HALO + start, count)
        return ref[lead + (at, 0)], ref[lead + (at, 1)]

    def put(ref, lead, start, count, value):
        at = pl.ds(HALO + start, count)
        ref[lead + (at, 0)] = value[0]
        ref[lead + (at, 1)] = value[1]

    def each(function, *values):
        return tuple(function(*parts) for parts in zip(*values))

    def sides(value):
        even, odd = value
        even_up, odd_up = pltpu.roll(even, LANES - 1, 2), pltpu.roll(odd, LANES - 1, 2)
        even_down, odd_down = pltpu.roll(even, 1, 2), pltpu.roll(odd, 1, 2)
        following = (
            jnp.where(is_last, odd_up, even_up),
            jnp.where(is_last, pltpu.roll(even_up, half - 1, 1), odd_up),
        )
        previous = (
            jnp.where(is_first, pltpu.roll(odd_down, 1, 1), even_down),
            jnp.where(is_first, even_down, odd_down),
        )
        return following, previous

    def col_diff(value):
        following, previous = sides(value)
        return each(lambda a, b: a - b, following, previous)

    def row_diff(value):
        return each(lambda a: a[2:] - a[:-2], value)

    def inner_rows(value):
        return each(lambda a: a[1:-1], value)

    up_scale = jnp.where(has_up, 1.0, 0.0)
    down_scale = jnp.where(has_down, 1.0, 0.0)

    def masked(value, start, count):
        if not isinstance(start, int) or (start >= 0 and start + count <= rows):
            return value
        scales = []
        for r in range(start, start + count):
            scales.append(up_scale if r < 0 else down_scale if r >= rows else None)

        def scale(part):
            return jnp.concatenate(
                [part[i:i + 1] if s is None else part[i:i + 1] * s for i, s in enumerate(scales)], 0
            )

        return each(scale, value)

    def field(step, f):
        return (S, (f,)) if step == 0 else (E, (step - 1, f))

    def height_stage(step, start, count):
        h_ref, h_at = field(step, 0)
        u_ref, u_at = field(step, 1)
        v_ref, v_at = field(step, 2)
        wide_d = get(S, (DEPTH,), start - 1, count + 2)
        flux_x = each(jnp.multiply, wide_d, get(u_ref, u_at, start - 1, count + 2))
        flux_y = each(jnp.multiply, inner_rows(wide_d), get(v_ref, v_at, start, count))
        h = get(h_ref, h_at, start, count)
        new_h = each(
            lambda a, x, y: a - (time_step * 0.5) * (x + y), h, row_diff(flux_x), col_diff(flux_y)
        )
        put(E, (step, 0), start, count, masked(new_h, start, count))

    def wind_stage(step, start, count):
        u_ref, u_at = field(step, 1)
        v_ref, v_at = field(step, 2)
        wide_h = get(E, (step, 0), start - 1, count + 2)
        u = get(u_ref, u_at, start, count)
        v = get(v_ref, v_at, start, count)
        pull, turn = time_step * gravity * 0.5, time_step * coriolis
        new_u = each(lambda a, b, x: a - pull * x + turn * b, u, v, row_diff(wide_h))
        new_v = each(lambda a, b, y: b - pull * y - turn * a, u, v, col_diff(inner_rows(wide_h)))
        if step == FSTEPS - 1:
            new_u, new_v = masked(new_u, start, count), masked(new_v, start, count)
        put(E, (step, 1), start, count, new_u)
        put(E, (step, 2), start, count, new_v)

    def spread_stage(step, start, count):
        kappa = get(S, (KAPPA,), start, count)
        rest = each(lambda k: 1.0 - 4.0 * k, kappa)
        for f in range(6):
            if step == 0:
                ref, at = field(FSTEPS, f - 3) if f >= 3 else field(0, f)
            else:
                ref, at = W, (step - 1, f)
            wide = get(ref, at, start - 1, count + 2)
            w = inner_rows(wide)
            following, previous = sides(w)
            new = each(
                lambda a, n, p, c, k, r: r * c + k * ((a[2:] + a[:-2]) + (n + p)),
                wide, following, previous, w, kappa, rest,
            )
            put(W, (step, f), start, count, new)

    stages = []
    for step in range(FSTEPS):
        stages.append((functools.partial(height_stage, step), HALO - 1 - 2 * step, 8))
        stages.append((functools.partial(wind_stage, step), HALO - 2 - 2 * step, 8))
    for step in range(DSTEPS):
        stages.append((functools.partial(spread_stage, step), DSTEPS - 1 - step, 8))

    def advance(stage, lo, hi, size):
        count = hi - lo
        whole = count // size
        if whole > 1:

            def body(i, carry):
                stage(lo + i * size, size)
                return carry

            for i in range(whole):
                body(i, 0)
            lo += whole * size
        elif whole == 1:
            stage(lo, size)
            lo += size
        if hi > lo:
            stage(lo, hi - lo)

    def compute(g):
        for stage, margin, size in stages:
            for lo, count, _ in pieces[g]:
                hi = lo + count
                if g == 0:
                    advance(stage, lo - margin, hi + margin, size)
                elif hi <= windows[0][0]:
                    advance(stage, lo - margin, hi - margin, size)
                else:
                    advance(stage, lo + margin, hi + margin, size)

    later = jnp.minimum(me + 1, subs - 1)
    keep = jnp.where(me < subs - 1, 1.0, 0.0)

    def weights(s):
        return mixing[s, me], mixing[s, later] * keep

    dest_pair = [lax.rem(pair + k, pairs) for k in range(pairs)]
    w_mine = [weights(q * 2 + parity) for q in dest_pair]
    w_mate = [weights(q * 2 + 1 - parity) for q in dest_pair]
    order = list(range(1, pairs)) + [0]

    def span(g):
        first = pieces[g][0][2]
        return pl.ds(first, sum(count for _, count, _ in pieces[g]))

    def a_copy(g, k):
        at = (k, slice(None), span(g))
        return pltpu.make_async_remote_copy(
            src_ref=send_a.at[at], dst_ref=recv_a.at[at],
            send_sem=a_send, recv_sem=a_recv.at[g, k],
            device_id={"sub": mate}, device_id_type=pl.DeviceIdType.MESH,
        )

    def b_copy(g, k):
        at = (k - 1, slice(None), span(g))
        return pltpu.make_async_remote_copy(
            src_ref=send_b.at[at], dst_ref=recv_b.at[at],
            send_sem=b_send, recv_sem=b_recv.at[g, k - 1],
            device_id={"sub": dest_pair[k] * 2 + parity},
            device_id_type=pl.DeviceIdType.MESH,
        )

    def terms(g):
        for k in order:
            for lo, count, place in pieces[g]:
                at = pl.ds(place, count)
                for f in range(3):
                    start = W[DSTEPS - 1, f, pl.ds(HALO + lo, count)]
                    end = W[DSTEPS - 1, 3 + f, pl.ds(HALO + lo, count)]
                    a, b = w_mate[k]
                    send_a[k, f, at] = a * start - b * end
                    a, b = w_mine[k]
                    mine = a * start - b * end
                    if k == 0:
                        M[f, at] = mine
                    else:
                        send_b[k - 1, f, at] = mine
            a_copy(g, k).start()

    def join(g):
        for k in range(1, pairs):
            a_copy(g, k).wait_recv()
            at = (k - 1, slice(None), span(g))
            send_b[at] = send_b[at] + recv_a[(k, slice(None), span(g))]
            b_copy(g, k).start()
        a_copy(g, 0).wait_recv()
        at = (slice(None), span(g))
        M[at] = M[at] + recv_a[(0,) + at]

    def finish(g):
        for k in range(1, pairs):
            b_copy(g, k).wait_recv()
        for lo, count, place in pieces[g]:
            for f in range(3):
                for i in range(count):
                    r = lo + i
                    total = M[f, place + i]
                    for k in range(1, pairs):
                        total = total + recv_b[k - 1, f, place + i]
                    base = (f * (rows // SUBLANES) + r // SUBLANES) * blocks * SUBLANES + r % SUBLANES
                    for e in range(2):
                        out[pl.ds(base + e * SUBLANES, half, stride=2 * SUBLANES), :] = total[e]

    enter()
    compute(0)
    terms(0)
    compute(1)
    terms(1)
    join(0)
    pass_land()
    join(1)
    take_land()
    for g in range(groups):
        take_halo(g)
        compute(g + 2)
        terms(g + 2)
        join(g + 2)
    for g in range(groups + 2):
        finish(g)

    pltpu.make_async_copy(send_a, send_a, a_send).wait()
    if pairs > 1:
        pltpu.make_async_copy(send_b, send_b, b_send).wait()
    sent = S.at[0, pl.ds(0, 3 * HALO - 2)]
    for way in range(2):

        @pl.when(goes[way])
        def _():
            wait_for(land_bytes, land_send.at[way])
            wait_for(sent, halo_send.at[way])

        @pl.when(comes[way])
        def _():
            wait_for(land_bytes, pass_send.at[way])


def solution(mesh):
    subs, tiles = mesh.shape["sub"], mesh.shape["tile"]

    def local(states, terrain, depth_table, spread_table, mixing):
        _, fields, rows, cols = states.shape
        pairs = subs // 2
        many = max(pairs - 1, 1)
        blocks = cols // LANES
        row = (2, blocks // 2, LANES)
        tall = rows + 2 * HALO
        dma = pltpu.SemaphoreType.DMA
        phases = len(windows_of(rows))
        vmem = pltpu.VMEM
        result = pl.pallas_call(
            functools.partial(kernel, subs, tiles, rows, cols, depth_table.shape[0]),
            out_shape=jax.ShapeDtypeStruct((fields * rows * blocks, LANES), jnp.float32),
            in_specs=[pl.BlockSpec(memory_space=pltpu.HBM)] * 5,
            out_specs=pl.BlockSpec(memory_space=pltpu.VMEM),
            scratch_shapes=[
                pltpu.SMEM(depth_table.shape, jnp.float32),
                pltpu.SMEM(spread_table.shape, jnp.float32),
                pltpu.SMEM(mixing.shape, jnp.float32),
                vmem((rows,) + row, jnp.int32),
                vmem((5, tall) + row, jnp.float32),
                vmem((FSTEPS, fields, tall) + row, jnp.float32),
                vmem((DSTEPS, 2 * fields, tall) + row, jnp.float32),
                vmem((pairs, fields, rows) + row, jnp.float32),
                vmem((pairs, fields, rows) + row, jnp.float32),
                vmem((many, fields, rows) + row, jnp.float32),
                vmem((many, fields, rows) + row, jnp.float32),
                vmem((fields, rows) + row, jnp.float32),
                dma((5,)),
                dma((2,)),
                dma((2,)),
                dma((2,)),
                dma((2,)),
                dma((2,)),
                dma((2, HALO // STEP)),
                dma(()),
                dma((phases, pairs)),
                dma(()),
                dma((phases, many)),
            ],
            compiler_params=pltpu.CompilerParams(
                collective_id=0, has_side_effects=True, vmem_limit_bytes=46 * 1024 * 1024
            ),
            name="gradient",
        )(
            *(
                pltpu.with_memory_space_constraint(value, pltpu.HBM)
                for value in (depth_table, spread_table, mixing, states, terrain)
            )
        )
        tiled = result.reshape(fields, rows // SUBLANES, blocks, SUBLANES, LANES)
        return tiled.transpose(0, 1, 3, 2, 4).reshape(states.shape)

    in_specs = (P("sub", None, "tile", None), P("tile", None), P(), P(), P())
    out_specs = P("sub", None, "tile", None)
    return jax.shard_map(local, mesh=mesh, in_specs=in_specs, out_specs=out_specs, check_vma=False)
```

```python
import functools

import jax
import jax.numpy as jnp
from jax import lax
from jax.experimental import pallas as pl
from jax.experimental.pallas import tpu as pltpu
from jax.sharding import PartitionSpec as P

FSTEPS = 3
DSTEPS = 3
time_step = 0.5
gravity = 1.0
coriolis = 0.3

LANES = 128
SUBLANES = 8
HALO = 2 * FSTEPS + DSTEPS
REACHES = (2, 5, 9)
DEPTH, KAPPA = 3, 4


def windows_of(rows):
    middle = rows // 2
    found = [(HALO, middle), (HALO, rows - HALO)]
    for reach in REACHES:
        found.append((HALO - reach, rows - HALO + reach))
    return found


def pieces_of(rows):
    last, place, pieces = None, 0, []
    for window in windows_of(rows):
        spans = [window] if last is None else [(window[0], last[0]), (last[1], window[1])]
        last = window
        held = []
        for lo, hi in spans:
            if hi > lo:
                held.append((lo, hi - lo, place))
                place += hi - lo
        pieces.append(held)
    return pieces


def kernel(
    subs, tiles, rows, cols, nclass,
    depth_in, spread_in, mixing_in, states, terrain, out,
    depth_tab, spread_tab, mixing, T, S, E, W, send_a, recv_a, send_b, recv_b, M,
    load_sem, tile_send, land_recv, pass_recv, halo_recv, a_send, a_recv, b_send, b_recv,
):
    pairs = subs // 2
    blocks = cols // LANES
    half = blocks // 2
    me = lax.axis_index("sub")
    tile = lax.axis_index("tile")
    parity = lax.rem(me, 2)
    mate = me + 1 - 2 * parity
    pair = me // 2
    has_up = tile > 0
    has_down = tile < tiles - 1
    up, down = tile - 1, tile + 1
    windows, pieces = windows_of(rows), pieces_of(rows)
    groups = len(REACHES)

    tables = [
        pltpu.make_async_copy(depth_in, depth_tab, load_sem.at[2]),
        pltpu.make_async_copy(spread_in, spread_tab, load_sem.at[3]),
        pltpu.make_async_copy(mixing_in, mixing, load_sem.at[4]),
    ]
    for copy in tables:
        copy.start()

    own = pl.ds(HALO, rows)
    pltpu.make_async_copy(terrain, T, load_sem.at[0]).start()
    for b in range(blocks):
        at = pl.ds(b * LANES, LANES)
        pltpu.make_async_copy(
            states.at[0, :, :, at], S.at[pl.ds(0, 3), own, b % 2, b // 2], load_sem.at[1]
        ).start()

    barrier = pltpu.get_barrier_semaphore()
    pl.semaphore_signal(barrier, inc=1, device_id={"sub": mate})
    for k in range(1, pairs):
        pl.semaphore_signal(
            barrier, inc=1, device_id={"sub": lax.rem(pair + k, pairs) * 2 + parity}
        )

    @pl.when(has_up)
    def _():
        pl.semaphore_signal(barrier, inc=1, device_id={"tile": up})

    @pl.when(has_down)
    def _():
        pl.semaphore_signal(barrier, inc=1, device_id={"tile": down})

    @pl.when(jnp.logical_not(has_up))
    def _():
        S[:, 0:HALO] = jnp.zeros((5, HALO, 2, half, LANES), jnp.float32)

    @pl.when(jnp.logical_not(has_down))
    def _():
        S[:, HALO + rows:] = jnp.zeros((5, HALO, 2, half, LANES), jnp.float32)

    pltpu.make_async_copy(T, T, load_sem.at[0]).wait()
    for copy in tables:
        copy.wait()
    def lookup(i, carry):
        for j in range(SUBLANES):
            for e in range(2):
                first = (i * blocks + e) * SUBLANES + j
                kind = T[pl.ds(first, half, stride=2 * SUBLANES), :]
                depth = jnp.zeros(kind.shape, jnp.float32)
                kappa = jnp.zeros(kind.shape, jnp.float32)
                for n in range(nclass):
                    hit = kind == n
                    depth = jnp.where(hit, depth_tab[n], depth)
                    kappa = jnp.where(hit, spread_tab[n], kappa)
                S[DEPTH, HALO + i * SUBLANES + j, e] = depth
                S[KAPPA, HALO + i * SUBLANES + j, e] = kappa
        return carry

    lax.fori_loop(0, rows // SUBLANES, lookup, 0)
    loaded = S.at[pl.ds(0, 3), own]
    pltpu.make_async_copy(loaded, loaded, load_sem.at[1]).wait()

    def edge(way, near, far):
        count = far - near + 1
        if way == 0:
            return pl.ds(HALO + rows - far, count), pl.ds(HALO - far, count)
        return pl.ds(HALO + near - 1, count), pl.ds(HALO + rows + near - 1, count)

    def to_tile(way, source, target, send, recv):
        return pltpu.make_async_remote_copy(
            src_ref=source, dst_ref=target, send_sem=send, recv_sem=recv,
            device_id={"tile": down if way == 0 else up}, device_id_type=pl.DeviceIdType.MESH,
        )

    land_rows = ((DEPTH, HALO), (KAPPA, DSTEPS - 1))
    land_bytes = S.at[0, pl.ds(0, HALO + DSTEPS - 1), 0]

    def land_copies(way):
        copies = []
        for f, far in land_rows:
            source, target = edge(way, 1, far)
            copies.append(to_tile(
                way, S.at[f, source, parity], S.at[f, target, parity],
                tile_send.at[way], land_recv.at[way],
            ))
        return copies

    def pass_copies(way):
        copies = []
        for f, far in land_rows:
            _, at = edge(way, 1, far)
            copies.append(pltpu.make_async_remote_copy(
                src_ref=S.at[f, at, parity], dst_ref=S.at[f, at, parity],
                send_sem=tile_send.at[1 - way], recv_sem=pass_recv.at[way],
                device_id={"sub": mate}, device_id_type=pl.DeviceIdType.MESH,
            ))
        return copies

    def halo_copies(way, g):
        near, far = (REACHES[g - 1] if g > 0 else 0) + 1, REACHES[g]
        parts = [(pl.ds(0, 3), near, far)]
        if g == groups - 1:
            parts = [(pl.ds(0, 3), near, far - 1), (pl.ds(1, 1), far, far)]
        copies = []
        for fields, first, last in parts:
            source, target = edge(way, first, last)
            copies.append(to_tile(
                way, S.at[fields, source], S.at[fields, target],
                tile_send.at[way], halo_recv.at[way, g],
            ))
        return copies

    def halo_bytes(g):
        count = REACHES[g] - (REACHES[g - 1] if g > 0 else 0)
        return S.at[0, pl.ds(0, 3 * count - (2 if g == groups - 1 else 0))]

    def wait_for(some, sem):
        pltpu.make_async_copy(some, some, sem).wait()

    comes = (has_up, has_down)
    goes = (has_down, has_up)

    def enter():
        pl.semaphore_wait(
            barrier, pairs + has_up.astype(jnp.int32) + has_down.astype(jnp.int32)
        )
    def send_land():
        for way in range(2):

            @pl.when(goes[way])
            def _():
                for copy in land_copies(way):
                    copy.start()

    def send_halo(g):
        for way in range(2):

            @pl.when(goes[way])
            def _():
                for copy in halo_copies(way, g):
                    copy.start()

    def pass_land():
        for way in range(2):

            @pl.when(comes[way])
            def _():
                wait_for(land_bytes, land_recv.at[way])
                for copy in pass_copies(way):
                    copy.start()

    def take_land():
        for way in range(2):

            @pl.when(comes[way])
            def _():
                wait_for(land_bytes, pass_recv.at[way])

    def take_halo(g):
        for way in range(2):

            @pl.when(comes[way])
            def _():
                wait_for(halo_bytes(g), halo_recv.at[way, g])

    lane = lax.broadcasted_iota(jnp.int32, (1, half, LANES), 2)
    is_first, is_last = lane == 0, lane == LANES - 1

    def get(ref, lead, start, count):
        at = pl.ds(HALO + start, count)
        return ref[lead + (at, 0)], ref[lead + (at, 1)]

    def put(ref, lead, start, count, value):
        at = pl.ds(HALO + start, count)
        ref[lead + (at, 0)] = value[0]
        ref[lead + (at, 1)] = value[1]

    def each(function, *values):
        return tuple(function(*parts) for parts in zip(*values))

    def sides(value):
        even, odd = value
        even_up, odd_up = pltpu.roll(even, LANES - 1, 2), pltpu.roll(odd, LANES - 1, 2)
        even_down, odd_down = pltpu.roll(even, 1, 2), pltpu.roll(odd, 1, 2)
        following = (
            jnp.where(is_last, odd_up, even_up),
            jnp.where(is_last, pltpu.roll(even_up, half - 1, 1), odd_up),
        )
        previous = (
            jnp.where(is_first, pltpu.roll(odd_down, 1, 1), even_down),
            jnp.where(is_first, even_down, odd_down),
        )
        return following, previous

    def col_diff(value):
        following, previous = sides(value)
        return each(lambda a, b: a - b, following, previous)

    def row_diff(value):
        return each(lambda a: a[2:] - a[:-2], value)

    def inner_rows(value):
        return each(lambda a: a[1:-1], value)

    up_scale = jnp.where(has_up, 1.0, 0.0)
    down_scale = jnp.where(has_down, 1.0, 0.0)

    def masked(value, start, count):
        if not isinstance(start, int) or (start >= 0 and start + count <= rows):
            return value
        scales = []
        for r in range(start, start + count):
            scales.append(up_scale if r < 0 else down_scale if r >= rows else None)

        def scale(part):
            return jnp.concatenate(
                [part[i:i + 1] if s is None else part[i:i + 1] * s for i, s in enumerate(scales)], 0
            )

        return each(scale, value)

    def field(step, f):
        return (S, (f,)) if step == 0 else (E, (step - 1, f))

    def height_stage(step, start, count):
        h_ref, h_at = field(step, 0)
        u_ref, u_at = field(step, 1)
        v_ref, v_at = field(step, 2)
        wide_d = get(S, (DEPTH,), start - 1, count + 2)
        flux_x = each(jnp.multiply, wide_d, get(u_ref, u_at, start - 1, count + 2))
        flux_y = each(jnp.multiply, inner_rows(wide_d), get(v_ref, v_at, start, count))
        h = get(h_ref, h_at, start, count)
        new_h = each(
            lambda a, x, y: a - (time_step * 0.5) * (x + y), h, row_diff(flux_x), col_diff(flux_y)
        )
        put(E, (step, 0), start, count, masked(new_h, start, count))

    def wind_stage(step, start, count):
        u_ref, u_at = field(step, 1)
        v_ref, v_at = field(step, 2)
        wide_h = get(E, (step, 0), start - 1, count + 2)
        u = get(u_ref, u_at, start, count)
        v = get(v_ref, v_at, start, count)
        pull, turn = time_step * gravity * 0.5, time_step * coriolis
        new_u = each(lambda a, b, x: a - pull * x + turn * b, u, v, row_diff(wide_h))
        new_v = each(lambda a, b, y: b - pull * y - turn * a, u, v, col_diff(inner_rows(wide_h)))
        if step == FSTEPS - 1:
            new_u, new_v = masked(new_u, start, count), masked(new_v, start, count)
        put(E, (step, 1), start, count, new_u)
        put(E, (step, 2), start, count, new_v)

    def spread_stage(step, start, count):
        kappa = get(S, (KAPPA,), start, count)
        rest = each(lambda k: 1.0 - 4.0 * k, kappa)
        for f in range(6):
            if step == 0:
                ref, at = field(FSTEPS, f - 3) if f >= 3 else field(0, f)
            else:
                ref, at = W, (step - 1, f)
            wide = get(ref, at, start - 1, count + 2)
            w = inner_rows(wide)
            following, previous = sides(w)
            new = each(
                lambda a, n, p, c, k, r: r * c + k * ((a[2:] + a[:-2]) + (n + p)),
                wide, following, previous, w, kappa, rest,
            )
            put(W, (step, f), start, count, new)

    stages = []
    for step in range(FSTEPS):
        stages.append((functools.partial(height_stage, step), HALO - 1 - 2 * step, 4))
        stages.append((functools.partial(wind_stage, step), HALO - 2 - 2 * step, 4))
    for step in range(DSTEPS):
        stages.append((functools.partial(spread_stage, step), DSTEPS - 1 - step, 4))

    def advance(stage, lo, hi, size):
        count = hi - lo
        whole = count // size
        if whole > 1:

            def body(i, carry):
                stage(lo + i * size, size)
                return carry

            for i in range(whole):
                body(i, 0)
            lo += whole * size
        elif whole == 1:
            stage(lo, size)
            lo += size
        if hi > lo:
            stage(lo, hi - lo)

    def compute(g):
        for stage, margin, size in stages:
            for lo, count, _ in pieces[g]:
                hi = lo + count
                if g == 0:
                    advance(stage, lo - margin, hi + margin, size)
                elif hi <= windows[0][0]:
                    advance(stage, lo - margin, hi - margin, size)
                else:
                    advance(stage, lo + margin, hi + margin, size)

    later = jnp.minimum(me + 1, subs - 1)
    keep = jnp.where(me < subs - 1, 1.0, 0.0)

    def weights(s):
        return mixing[s, me], mixing[s, later] * keep

    dest_pair = [lax.rem(pair + k, pairs) for k in range(pairs)]
    w_mine = [weights(q * 2 + parity) for q in dest_pair]
    w_mate = [weights(q * 2 + 1 - parity) for q in dest_pair]
    order = list(range(1, pairs)) + [0]

    def span(g):
        first = pieces[g][0][2]
        return pl.ds(first, sum(count for _, count, _ in pieces[g]))

    def a_copy(g, k):
        at = (k, slice(None), span(g))
        return pltpu.make_async_remote_copy(
            src_ref=send_a.at[at], dst_ref=recv_a.at[at],
            send_sem=a_send, recv_sem=a_recv.at[g, k],
            device_id={"sub": mate}, device_id_type=pl.DeviceIdType.MESH,
        )

    def b_copy(g, k):
        at = (k - 1, slice(None), span(g))
        return pltpu.make_async_remote_copy(
            src_ref=send_b.at[at], dst_ref=recv_b.at[at],
            send_sem=b_send, recv_sem=b_recv.at[g, k - 1],
            device_id={"sub": dest_pair[k] * 2 + parity},
            device_id_type=pl.DeviceIdType.MESH,
        )

    def terms(g):
        for k in order:
            for lo, count, place in pieces[g]:
                at = pl.ds(place, count)
                for f in range(3):
                    start = W[DSTEPS - 1, f, pl.ds(HALO + lo, count)]
                    end = W[DSTEPS - 1, 3 + f, pl.ds(HALO + lo, count)]
                    a, b = w_mate[k]
                    send_a[k, f, at] = a * start - b * end
                    a, b = w_mine[k]
                    mine = a * start - b * end
                    if k == 0:
                        M[f, at] = mine
                    else:
                        send_b[k - 1, f, at] = mine
            a_copy(g, k).start()

    def join(g):
        for k in range(1, pairs):
            a_copy(g, k).wait_recv()
            at = (k - 1, slice(None), span(g))
            send_b[at] = send_b[at] + recv_a[(k, slice(None), span(g))]
            b_copy(g, k).start()
        a_copy(g, 0).wait_recv()
        at = (slice(None), span(g))
        M[at] = M[at] + recv_a[(0,) + at]

    def finish(g):
        for k in range(1, pairs):
            b_copy(g, k).wait_recv()
        for lo, count, place in pieces[g]:
            for f in range(3):
                for i in range(count):
                    r = lo + i
                    total = M[f, place + i]
                    for k in range(1, pairs):
                        total = total + recv_b[k - 1, f, place + i]
                    base = (f * (rows // SUBLANES) + r // SUBLANES) * blocks * SUBLANES + r % SUBLANES
                    for e in range(2):
                        out[pl.ds(base + e * SUBLANES, half, stride=2 * SUBLANES), :] = total[e]

    enter()
    send_land()
    send_halo(0)
    compute(0)
    terms(0)
    join(0)
    send_halo(1)
    compute(1)
    terms(1)
    pass_land()
    for g in range(2, groups):
        send_halo(g)
    join(1)
    take_land()
    for g in range(groups):
        take_halo(g)
        compute(g + 2)
        terms(g + 2)
        join(g + 2)
    for g in range(groups + 2):
        finish(g)

    pltpu.make_async_copy(send_a, send_a, a_send).wait()
    if pairs > 1:
        pltpu.make_async_copy(send_b, send_b, b_send).wait()
    sent = S.at[0, pl.ds(0, 3 * HALO - 2 + HALO + DSTEPS - 1)]
    for way in range(2):

        @pl.when(goes[way])
        def _():
            wait_for(sent, tile_send.at[way])


def solution(mesh):
    subs, tiles = mesh.shape["sub"], mesh.shape["tile"]

    def local(states, terrain, depth_table, spread_table, mixing):
        _, fields, rows, cols = states.shape
        pairs = subs // 2
        many = max(pairs - 1, 1)
        blocks = cols // LANES
        row = (2, blocks // 2, LANES)
        tall = rows + 2 * HALO
        dma = pltpu.SemaphoreType.DMA
        phases = len(windows_of(rows))
        vmem = pltpu.VMEM

        def flat(value):
            tiles_last = value.reshape(rows // SUBLANES, SUBLANES, blocks, LANES)
            return tiles_last.transpose(0, 2, 1, 3).reshape(-1, LANES)

        result = pl.pallas_call(
            functools.partial(kernel, subs, tiles, rows, cols, depth_table.shape[0]),
            out_shape=jax.ShapeDtypeStruct((fields * rows * blocks, LANES), jnp.float32),
            in_specs=[pl.BlockSpec(memory_space=pltpu.HBM)] * 5,
            out_specs=pl.BlockSpec(memory_space=pltpu.VMEM),
            scratch_shapes=[
                pltpu.SMEM(depth_table.shape, jnp.float32),
                pltpu.SMEM(spread_table.shape, jnp.float32),
                pltpu.SMEM(mixing.shape, jnp.float32),
                vmem((rows * blocks, LANES), jnp.int32),
                vmem((5, tall) + row, jnp.float32),
                vmem((FSTEPS, fields, tall) + row, jnp.float32),
                vmem((DSTEPS, 2 * fields, tall) + row, jnp.float32),
                vmem((pairs, fields, rows) + row, jnp.float32),
                vmem((pairs, fields, rows) + row, jnp.float32),
                vmem((many, fields, rows) + row, jnp.float32),
                vmem((many, fields, rows) + row, jnp.float32),
                vmem((fields, rows) + row, jnp.float32),
                dma((5,)),
                dma((2,)),
                dma((2,)),
                dma((2,)),
                dma((2, len(REACHES))),
                dma(()),
                dma((phases, pairs)),
                dma(()),
                dma((phases, many)),
            ],
            compiler_params=pltpu.CompilerParams(
                collective_id=0, has_side_effects=True, vmem_limit_bytes=46 * 1024 * 1024
            ),
            name="gradient",
        )(
            *(
                pltpu.with_memory_space_constraint(value, pltpu.HBM)
                for value in (depth_table, spread_table, mixing, states, flat(terrain))
            )
        )
        tiled = result.reshape(fields, rows // SUBLANES, blocks, SUBLANES, LANES)
        return tiled.transpose(0, 1, 3, 2, 4).reshape(states.shape)

    in_specs = (P("sub", None, "tile", None), P("tile", None), P(), P(), P())
    out_specs = P("sub", None, "tile", None)
    return jax.shard_map(local, mesh=mesh, in_specs=in_specs, out_specs=out_specs, check_vma=False)
```

```python
import functools

import jax
import jax.numpy as jnp
from jax import lax
from jax.experimental import pallas as pl
from jax.experimental.pallas import tpu as pltpu
from jax.sharding import PartitionSpec as P

FSTEPS = 3
DSTEPS = 3
time_step = 0.5
gravity = 1.0
coriolis = 0.3

LANES = 128
SUBLANES = 8
HALO = 2 * FSTEPS + DSTEPS
REACHES = (1, 3, 5, 9)
DEPTH, KAPPA = 3, 4


def windows_of(rows):
    middle = rows // 2
    found = [(HALO, middle), (HALO, rows - HALO)]
    for reach in REACHES:
        found.append((HALO - reach, rows - HALO + reach))
    return found


def pieces_of(rows):
    last, place, pieces = None, 0, []
    for window in windows_of(rows):
        spans = [window] if last is None else [(window[0], last[0]), (last[1], window[1])]
        last = window
        held = []
        for lo, hi in spans:
            if hi > lo:
                held.append((lo, hi - lo, place))
                place += hi - lo
        pieces.append(held)
    return pieces


def kernel(
    subs, tiles, rows, cols, nclass,
    depth_in, spread_in, mixing_in, states, terrain, out,
    depth_tab, spread_tab, mixing, T, S, E, W, Z, send_a, recv_a, send_b, recv_b, M,
    load_sem, tile_send, land_recv, pass_recv, halo_recv, a_send, a_recv, b_send, b_recv,
):
    pairs = subs // 2
    blocks = cols // LANES
    half = blocks // 2
    me = lax.axis_index("sub")
    tile = lax.axis_index("tile")
    parity = lax.rem(me, 2)
    mate = me + 1 - 2 * parity
    pair = me // 2
    has_up = tile > 0
    has_down = tile < tiles - 1
    up, down = tile - 1, tile + 1
    windows, pieces = windows_of(rows), pieces_of(rows)
    groups = len(REACHES)

    tables = [
        pltpu.make_async_copy(depth_in, depth_tab, load_sem.at[2]),
        pltpu.make_async_copy(spread_in, spread_tab, load_sem.at[3]),
        pltpu.make_async_copy(mixing_in, mixing, load_sem.at[4]),
    ]
    for copy in tables:
        copy.start()

    own = pl.ds(HALO, rows)
    pltpu.make_async_copy(terrain, T, load_sem.at[0]).start()
    for b in range(blocks):
        at = pl.ds(b * LANES, LANES)
        pltpu.make_async_copy(
            states.at[0, :, :, at], S.at[pl.ds(0, 3), own, b % 2, b // 2], load_sem.at[1]
        ).start()

    barrier = pltpu.get_barrier_semaphore()
    pl.semaphore_signal(barrier, inc=1, device_id={"sub": mate})
    for k in range(1, pairs):
        pl.semaphore_signal(
            barrier, inc=1, device_id={"sub": lax.rem(pair + k, pairs) * 2 + parity}
        )

    @pl.when(has_up)
    def _():
        pl.semaphore_signal(barrier, inc=1, device_id={"tile": up})

    @pl.when(has_down)
    def _():
        pl.semaphore_signal(barrier, inc=1, device_id={"tile": down})

    @pl.when(jnp.logical_not(has_up))
    def _():
        S[:, 0:HALO] = jnp.zeros((5, HALO, 2, half, LANES), jnp.float32)

    @pl.when(jnp.logical_not(has_down))
    def _():
        S[:, HALO + rows:] = jnp.zeros((5, HALO, 2, half, LANES), jnp.float32)

    pltpu.make_async_copy(T, T, load_sem.at[0]).wait()
    for copy in tables:
        copy.wait()
    def lookup(i, carry):
        for j in range(SUBLANES):
            for e in range(2):
                first = (i * blocks + e) * SUBLANES + j
                kind = T[pl.ds(first, half, stride=2 * SUBLANES), :]
                depth = jnp.zeros(kind.shape, jnp.float32)
                kappa = jnp.zeros(kind.shape, jnp.float32)
                for n in range(nclass):
                    hit = kind == n
                    depth = jnp.where(hit, depth_tab[n], depth)
                    kappa = jnp.where(hit, spread_tab[n], kappa)
                S[DEPTH, HALO + i * SUBLANES + j, e] = depth
                S[KAPPA, HALO + i * SUBLANES + j, e] = kappa
        return carry

    lax.fori_loop(0, rows // SUBLANES, lookup, 0)
    loaded = S.at[pl.ds(0, 3), own]
    pltpu.make_async_copy(loaded, loaded, load_sem.at[1]).wait()

    def edge(way, near, far):
        count = far - near + 1
        if way == 0:
            return pl.ds(HALO + rows - far, count), pl.ds(HALO - far, count)
        return pl.ds(HALO + near - 1, count), pl.ds(HALO + rows + near - 1, count)

    def to_tile(way, source, target, send, recv):
        return pltpu.make_async_remote_copy(
            src_ref=source, dst_ref=target, send_sem=send, recv_sem=recv,
            device_id={"tile": down if way == 0 else up}, device_id_type=pl.DeviceIdType.MESH,
        )

    land_rows = ((DEPTH, HALO), (KAPPA, DSTEPS - 1))
    land_bytes = S.at[0, pl.ds(0, HALO + DSTEPS - 1), 0]

    def land_copies(way):
        copies = []
        for f, far in land_rows:
            source, target = edge(way, 1, far)
            copies.append(to_tile(
                way, S.at[f, source, parity], S.at[f, target, parity],
                tile_send.at[way], land_recv.at[way],
            ))
        return copies

    def pass_copies(way):
        copies = []
        for f, far in land_rows:
            _, at = edge(way, 1, far)
            copies.append(pltpu.make_async_remote_copy(
                src_ref=S.at[f, at, parity], dst_ref=S.at[f, at, parity],
                send_sem=tile_send.at[1 - way], recv_sem=pass_recv.at[way],
                device_id={"sub": mate}, device_id_type=pl.DeviceIdType.MESH,
            ))
        return copies

    def halo_copies(way, g):
        near, far = (REACHES[g - 1] if g > 0 else 0) + 1, REACHES[g]
        parts = [(pl.ds(0, 3), near, far)]
        if g == groups - 1:
            parts = [(pl.ds(0, 3), near, far - 1), (pl.ds(1, 1), far, far)]
        copies = []
        for fields, first, last in parts:
            source, target = edge(way, first, last)
            copies.append(to_tile(
                way, S.at[fields, source], S.at[fields, target],
                tile_send.at[way], halo_recv.at[way, g],
            ))
        return copies

    def halo_bytes(g):
        count = REACHES[g] - (REACHES[g - 1] if g > 0 else 0)
        return S.at[0, pl.ds(0, 3 * count - (2 if g == groups - 1 else 0))]

    def wait_for(some, sem):
        pltpu.make_async_copy(some, some, sem).wait()

    comes = (has_up, has_down)
    goes = (has_down, has_up)

    def enter():
        pl.semaphore_wait(
            barrier, pairs + has_up.astype(jnp.int32) + has_down.astype(jnp.int32)
        )
    def send_land():
        for way in range(2):

            @pl.when(goes[way])
            def _():
                for copy in land_copies(way):
                    copy.start()

    def send_halo(g):
        for way in range(2):

            @pl.when(goes[way])
            def _():
                for copy in halo_copies(way, g):
                    copy.start()

    def pass_land():
        for way in range(2):

            @pl.when(comes[way])
            def _():
                wait_for(land_bytes, land_recv.at[way])
                for copy in pass_copies(way):
                    copy.start()

    def take_land():
        for way in range(2):

            @pl.when(comes[way])
            def _():
                wait_for(land_bytes, pass_recv.at[way])

    def take_halo(g):
        for way in range(2):

            @pl.when(comes[way])
            def _():
                wait_for(halo_bytes(g), halo_recv.at[way, g])

    lane = lax.broadcasted_iota(jnp.int32, (1, half, LANES), 2)
    is_first, is_last = lane == 0, lane == LANES - 1

    def get(ref, lead, start, count):
        at = pl.ds(HALO + start, count)
        return ref[lead + (at, 0)], ref[lead + (at, 1)]

    def put(ref, lead, start, count, value):
        at = pl.ds(HALO + start, count)
        ref[lead + (at, 0)] = value[0]
        ref[lead + (at, 1)] = value[1]

    def each(function, *values):
        return tuple(function(*parts) for parts in zip(*values))

    def sides(value):
        even, odd = value
        even_up, odd_up = pltpu.roll(even, LANES - 1, 2), pltpu.roll(odd, LANES - 1, 2)
        even_down, odd_down = pltpu.roll(even, 1, 2), pltpu.roll(odd, 1, 2)
        following = (
            jnp.where(is_last, odd_up, even_up),
            jnp.where(is_last, pltpu.roll(even_up, half - 1, 1), odd_up),
        )
        previous = (
            jnp.where(is_first, pltpu.roll(odd_down, 1, 1), even_down),
            jnp.where(is_first, even_down, odd_down),
        )
        return following, previous

    def col_diff(value):
        following, previous = sides(value)
        return each(lambda a, b: a - b, following, previous)

    def row_diff(value):
        return each(lambda a: a[2:] - a[:-2], value)

    def inner_rows(value):
        return each(lambda a: a[1:-1], value)

    up_scale = jnp.where(has_up, 1.0, 0.0)
    down_scale = jnp.where(has_down, 1.0, 0.0)

    def masked(value, start, count):
        if not isinstance(start, int) or (start >= 0 and start + count <= rows):
            return value
        scales = []
        for r in range(start, start + count):
            scales.append(up_scale if r < 0 else down_scale if r >= rows else None)

        def scale(part):
            return jnp.concatenate(
                [part[i:i + 1] if s is None else part[i:i + 1] * s for i, s in enumerate(scales)], 0
            )

        return each(scale, value)

    def field(step, f):
        return (S, (f,)) if step == 0 else (E, (step - 1, f))

    def height_stage(step, start, count):
        h_ref, h_at = field(step, 0)
        u_ref, u_at = field(step, 1)
        v_ref, v_at = field(step, 2)
        wide_d = get(S, (DEPTH,), start - 1, count + 2)
        flux_x = each(jnp.multiply, wide_d, get(u_ref, u_at, start - 1, count + 2))
        flux_y = each(jnp.multiply, inner_rows(wide_d), get(v_ref, v_at, start, count))
        h = get(h_ref, h_at, start, count)
        new_h = each(
            lambda a, x, y: a - (time_step * 0.5) * (x + y), h, row_diff(flux_x), col_diff(flux_y)
        )
        put(E, (step, 0), start, count, masked(new_h, start, count))

    def wind_stage(step, start, count):
        u_ref, u_at = field(step, 1)
        v_ref, v_at = field(step, 2)
        wide_h = get(E, (step, 0), start - 1, count + 2)
        u = get(u_ref, u_at, start, count)
        v = get(v_ref, v_at, start, count)
        pull, turn = time_step * gravity * 0.5, time_step * coriolis
        new_u = each(lambda a, b, x: a - pull * x + turn * b, u, v, row_diff(wide_h))
        new_v = each(lambda a, b, y: b - pull * y - turn * a, u, v, col_diff(inner_rows(wide_h)))
        if step == FSTEPS - 1:
            new_u, new_v = masked(new_u, start, count), masked(new_v, start, count)
        put(E, (step, 1), start, count, new_u)
        put(E, (step, 2), start, count, new_v)

    def spread(ref, at, start, count, kappa, rest):
        wide = get(ref, at, start - 1, count + 2)
        w = inner_rows(wide)
        following, previous = sides(w)
        return each(
            lambda a, n, p, c, k, r: r * c + k * ((a[2:] + a[:-2]) + (n + p)),
            wide, following, previous, w, kappa, rest,
        )

    def coefficients(start, count):
        kappa = get(S, (KAPPA,), start, count)
        return kappa, each(lambda k: 1.0 - 4.0 * k, kappa)

    def spread_stage(step, start, count):
        kappa, rest = coefficients(start, count)
        for f in range(6):
            if step == 0:
                ref, at = field(FSTEPS, f - 3) if f >= 3 else field(0, f)
            else:
                ref, at = W, (step - 1, f)
            put(W, (step, f), start, count, spread(ref, at, start, count, kappa, rest))

    stages = []
    for step in range(FSTEPS):
        stages.append((functools.partial(height_stage, step), HALO - 1 - 2 * step, 4))
        stages.append((functools.partial(wind_stage, step), HALO - 2 - 2 * step, 4))
    for step in range(DSTEPS):
        stages.append((functools.partial(spread_stage, step), DSTEPS - 1 - step, 4))

    def advance(stage, lo, hi, size):
        count = hi - lo
        whole = count // size
        if whole > 1:

            def body(i, carry):
                stage(lo + i * size, size)
                return carry

            for i in range(whole):
                body(i, 0)
            lo += whole * size
        elif whole == 1:
            stage(lo, size)
            lo += size
        if hi > lo:
            stage(lo, hi - lo)

    def compute(g, chosen=stages):
        for stage, margin, size in chosen:
            for lo, count, _ in pieces[g]:
                hi = lo + count
                if g == 0:
                    advance(stage, lo - margin, hi + margin, size)
                elif hi <= windows[0][0]:
                    advance(stage, lo - margin, hi - margin, size)
                else:
                    advance(stage, lo + margin, hi + margin, size)

    moves, spreads = stages[:2 * FSTEPS], stages[2 * FSTEPS:]

    def spread_inner():
        lo, hi = windows[1]
        for stage, margin, size in spreads:
            advance(stage, lo - margin, hi + margin, size)

    later = jnp.minimum(me + 1, subs - 1)
    keep = jnp.where(me < subs - 1, 1.0, 0.0)

    def weights(s):
        return mixing[s, me], mixing[s, later] * keep

    dest_pair = [lax.rem(pair + k, pairs) for k in range(pairs)]
    w_mine = [weights(q * 2 + parity) for q in dest_pair]
    w_mate = [weights(q * 2 + 1 - parity) for q in dest_pair]
    order = list(range(1, pairs)) + [0]

    def span(g):
        first = pieces[g][0][2]
        return pl.ds(first, sum(count for _, count, _ in pieces[g]))

    def a_copy(g, k):
        at = (k, slice(None), span(g))
        return pltpu.make_async_remote_copy(
            src_ref=send_a.at[at], dst_ref=recv_a.at[at],
            send_sem=a_send, recv_sem=a_recv.at[g, k],
            device_id={"sub": mate}, device_id_type=pl.DeviceIdType.MESH,
        )

    def b_copy(g, k):
        at = (k - 1, slice(None), span(g))
        return pltpu.make_async_remote_copy(
            src_ref=send_b.at[at], dst_ref=recv_b.at[at],
            send_sem=b_send, recv_sem=b_recv.at[g, k - 1],
            device_id={"sub": dest_pair[k] * 2 + parity},
            device_id_type=pl.DeviceIdType.MESH,
        )

    def mix_first(weight, ref, k):
        (lo, count, place), = pieces[0]
        a, b = weight

        def mix(start, n):
            for f in range(3):
                ref_end, at_end = field(FSTEPS, f)
                ends = get(ref_end, at_end, start, n)
                put(Z, (0, f), start, n, each(lambda x, y: a * x - b * y, get(S, (f,), start, n), ends))

        def spread_mixed(step, start, n):
            kappa, rest = coefficients(start, n)
            for f in range(3):
                new = spread(Z, (step, f), start, n, kappa, rest)
                if step < DSTEPS - 1:
                    put(Z, (step + 1, f), start, n, new)
                else:
                    for e in range(2):
                        ref[k, f, pl.ds(place + start - lo, n), e] = new[e]

        advance(mix, lo - DSTEPS, lo + count + DSTEPS, 4)
        for step in range(DSTEPS):
            margin = DSTEPS - 1 - step
            advance(functools.partial(spread_mixed, step), lo - margin, lo + count + margin, 4)

    def mate_terms(g, k):
        for lo, count, place in pieces[g]:
            at = pl.ds(place, count)
            for f in range(3):
                start = W[DSTEPS - 1, f, pl.ds(HALO + lo, count)]
                end = W[DSTEPS - 1, 3 + f, pl.ds(HALO + lo, count)]
                a, b = w_mate[k]
                send_a[k, f, at] = a * start - b * end
        a_copy(g, k).start()

    def own_terms(g, k):
        for lo, count, place in pieces[g]:
            at = pl.ds(place, count)
            for f in range(3):
                start = W[DSTEPS - 1, f, pl.ds(HALO + lo, count)]
                end = W[DSTEPS - 1, 3 + f, pl.ds(HALO + lo, count)]
                a, b = w_mine[k]
                mine = a * start - b * end
                if k == 0:
                    M[f, at] = mine
                else:
                    send_b[k - 1, f, at] = mine

    def terms(g):
        for k in order:
            mate_terms(g, k)
        for k in order:
            own_terms(g, k)

    def join(g):
        for k in range(1, pairs):
            a_copy(g, k).wait_recv()
            at = (k - 1, slice(None), span(g))
            send_b[at] = send_b[at] + recv_a[(k, slice(None), span(g))]
            b_copy(g, k).start()

    def finish(g):
        a_copy(g, 0).wait_recv()
        for k in range(1, pairs):
            b_copy(g, k).wait_recv()
        for lo, count, place in pieces[g]:
            for f in range(3):
                for i in range(count):
                    r = lo + i
                    total = M[f, place + i] + recv_a[0, f, place + i]
                    for k in range(1, pairs):
                        total = total + recv_b[k - 1, f, place + i]
                    base = (f * (rows // SUBLANES) + r // SUBLANES) * blocks * SUBLANES + r % SUBLANES
                    for e in range(2):
                        out[pl.ds(base + e * SUBLANES, half, stride=2 * SUBLANES), :] = total[e]

    enter()
    send_land()
    send_halo(0)
    if pairs == 2:
        compute(0, moves)
        mix_first(w_mate[1], send_a, 1)
        a_copy(0, 1).start()
        mix_first(w_mine[1], send_b, 0)
        join(0)
        send_halo(1)
        compute(1, moves)
        spread_inner()
        terms(1)
    else:
        compute(0)
        terms(0)
        join(0)
        send_halo(1)
        compute(1)
        terms(1)
    pass_land()
    for g in range(2, groups):
        send_halo(g)
    join(1)
    if pairs == 2:
        mate_terms(0, 0)
        own_terms(0, 0)
    take_land()
    for g in range(groups):
        take_halo(g)
        compute(g + 2)
        terms(g + 2)
        join(g + 2)
    for g in range(groups + 2):
        finish(g)

    pltpu.make_async_copy(send_a, send_a, a_send).wait()
    if pairs > 1:
        pltpu.make_async_copy(send_b, send_b, b_send).wait()
    sent = S.at[0, pl.ds(0, 3 * HALO - 2 + HALO + DSTEPS - 1)]
    for way in range(2):

        @pl.when(goes[way])
        def _():
            wait_for(sent, tile_send.at[way])


def solution(mesh):
    subs, tiles = mesh.shape["sub"], mesh.shape["tile"]

    def local(states, terrain, depth_table, spread_table, mixing):
        _, fields, rows, cols = states.shape
        pairs = subs // 2
        many = max(pairs - 1, 1)
        blocks = cols // LANES
        row = (2, blocks // 2, LANES)
        tall = rows + 2 * HALO
        dma = pltpu.SemaphoreType.DMA
        phases = len(windows_of(rows))
        vmem = pltpu.VMEM

        def flat(value):
            tiles_last = value.reshape(rows // SUBLANES, SUBLANES, blocks, LANES)
            return tiles_last.transpose(0, 2, 1, 3).reshape(-1, LANES)

        result = pl.pallas_call(
            functools.partial(kernel, subs, tiles, rows, cols, depth_table.shape[0]),
            out_shape=jax.ShapeDtypeStruct((fields * rows * blocks, LANES), jnp.float32),
            in_specs=[pl.BlockSpec(memory_space=pltpu.HBM)] * 5,
            out_specs=pl.BlockSpec(memory_space=pltpu.VMEM),
            scratch_shapes=[
                pltpu.SMEM(depth_table.shape, jnp.float32),
                pltpu.SMEM(spread_table.shape, jnp.float32),
                pltpu.SMEM(mixing.shape, jnp.float32),
                vmem((rows * blocks, LANES), jnp.int32),
                vmem((5, tall) + row, jnp.float32),
                vmem((FSTEPS, fields, tall) + row, jnp.float32),
                vmem((DSTEPS, 2 * fields, tall) + row, jnp.float32),
                vmem((DSTEPS, fields, tall) + row, jnp.float32),
                vmem((pairs, fields, rows) + row, jnp.float32),
                vmem((pairs, fields, rows) + row, jnp.float32),
                vmem((many, fields, rows) + row, jnp.float32),
                vmem((many, fields, rows) + row, jnp.float32),
                vmem((fields, rows) + row, jnp.float32),
                dma((5,)),
                dma((2,)),
                dma((2,)),
                dma((2,)),
                dma((2, len(REACHES))),
                dma(()),
                dma((phases, pairs)),
                dma(()),
                dma((phases, many)),
            ],
            compiler_params=pltpu.CompilerParams(
                collective_id=0, has_side_effects=True, vmem_limit_bytes=46 * 1024 * 1024
            ),
            name="gradient",
        )(
            *(
                pltpu.with_memory_space_constraint(value, pltpu.HBM)
                for value in (depth_table, spread_table, mixing, states, flat(terrain))
            )
        )
        tiled = result.reshape(fields, rows // SUBLANES, blocks, SUBLANES, LANES)
        return tiled.transpose(0, 1, 3, 2, 4).reshape(states.shape)

    in_specs = (P("sub", None, "tile", None), P("tile", None), P(), P(), P())
    out_specs = P("sub", None, "tile", None)
    return jax.shard_map(local, mesh=mesh, in_specs=in_specs, out_specs=out_specs, check_vma=False)
```

```python
import functools

import jax
import jax.numpy as jnp
from jax import lax
from jax.experimental import pallas as pl
from jax.experimental.pallas import tpu as pltpu
from jax.sharding import PartitionSpec as P

FSTEPS = 3
DSTEPS = 3
time_step = 0.5
gravity = 1.0
coriolis = 0.3

LANES = 128
SUBLANES = 8
HALO = 2 * FSTEPS + DSTEPS
REACHES = (2, 4, 7, 9)
DEPTH, KAPPA = 3, 4


def windows_of(rows):
    middle = rows // 2
    found = [(HALO, middle), (HALO, rows - HALO)]
    for reach in REACHES:
        found.append((HALO - reach, rows - HALO + reach))
    return found


def pieces_of(rows):
    last, place, pieces = None, 0, []
    for window in windows_of(rows):
        spans = [window] if last is None else [(window[0], last[0]), (last[1], window[1])]
        last = window
        held = []
        for lo, hi in spans:
            if hi > lo:
                held.append((lo, hi - lo, place))
                place += hi - lo
        pieces.append(held)
    return pieces


def kernel(
    subs, tiles, rows, cols, nclass,
    depth_in, spread_in, mixing_in, states, terrain, out,
    depth_tab, spread_tab, mixing, T, S, E, W, Z, send_a, recv_a, send_b, recv_b, M,
    load_sem, tile_send, land_recv, pass_recv, halo_recv, a_send, a_recv, b_send, b_recv,
):
    pairs = subs // 2
    blocks = cols // LANES
    half = blocks // 2
    me = lax.axis_index("sub")
    tile = lax.axis_index("tile")
    parity = lax.rem(me, 2)
    mate = me + 1 - 2 * parity
    pair = me // 2
    has_up = tile > 0
    has_down = tile < tiles - 1
    up, down = tile - 1, tile + 1
    windows, pieces = windows_of(rows), pieces_of(rows)
    groups = len(REACHES)

    tables = [
        pltpu.make_async_copy(depth_in, depth_tab, load_sem.at[2]),
        pltpu.make_async_copy(spread_in, spread_tab, load_sem.at[3]),
        pltpu.make_async_copy(mixing_in, mixing, load_sem.at[4]),
    ]
    own = pl.ds(HALO, rows)
    pltpu.make_async_copy(terrain, T, load_sem.at[0]).start()
    for copy in tables:
        copy.start()
    for b in range(blocks):
        at = pl.ds(b * LANES, LANES)
        pltpu.make_async_copy(
            states.at[0, :, :, at], S.at[pl.ds(0, 3), own, b % 2, b // 2], load_sem.at[1]
        ).start()

    barrier = pltpu.get_barrier_semaphore()
    pl.semaphore_signal(barrier, inc=1, device_id={"sub": mate})
    for k in range(1, pairs):
        pl.semaphore_signal(
            barrier, inc=1, device_id={"sub": lax.rem(pair + k, pairs) * 2 + parity}
        )

    @pl.when(has_up)
    def _():
        pl.semaphore_signal(barrier, inc=1, device_id={"tile": up})

    @pl.when(has_down)
    def _():
        pl.semaphore_signal(barrier, inc=1, device_id={"tile": down})

    @pl.when(jnp.logical_not(has_up))
    def _():
        S[:, 0:HALO] = jnp.zeros((5, HALO, 2, half, LANES), jnp.float32)

    @pl.when(jnp.logical_not(has_down))
    def _():
        S[:, HALO + rows:] = jnp.zeros((5, HALO, 2, half, LANES), jnp.float32)

    pltpu.make_async_copy(T, T, load_sem.at[0]).wait()
    for copy in tables:
        copy.wait()
    def lookup(i, carry):
        for j in range(SUBLANES):
            for e in range(2):
                first = (i * blocks + e) * SUBLANES + j
                kind = T[pl.ds(first, half, stride=2 * SUBLANES), :]
                depth = jnp.zeros(kind.shape, jnp.float32)
                kappa = jnp.zeros(kind.shape, jnp.float32)
                for n in range(nclass):
                    hit = kind == n
                    depth = jnp.where(hit, depth_tab[n], depth)
                    kappa = jnp.where(hit, spread_tab[n], kappa)
                S[DEPTH, HALO + i * SUBLANES + j, e] = depth
                S[KAPPA, HALO + i * SUBLANES + j, e] = kappa
        return carry

    lax.fori_loop(0, rows // SUBLANES, lookup, 0)
    loaded = S.at[pl.ds(0, 3), own]
    pltpu.make_async_copy(loaded, loaded, load_sem.at[1]).wait()

    def edge(way, near, far):
        count = far - near + 1
        if way == 0:
            return pl.ds(HALO + rows - far, count), pl.ds(HALO - far, count)
        return pl.ds(HALO + near - 1, count), pl.ds(HALO + rows + near - 1, count)

    def to_tile(way, source, target, send, recv):
        return pltpu.make_async_remote_copy(
            src_ref=source, dst_ref=target, send_sem=send, recv_sem=recv,
            device_id={"tile": down if way == 0 else up}, device_id_type=pl.DeviceIdType.MESH,
        )

    land_rows = ((DEPTH, HALO), (KAPPA, DSTEPS - 1))
    land_bytes = S.at[0, pl.ds(0, HALO + DSTEPS - 1), 0]

    def land_copies(way):
        copies = []
        for f, far in land_rows:
            source, target = edge(way, 1, far)
            copies.append(to_tile(
                way, S.at[f, source, parity], S.at[f, target, parity],
                tile_send.at[way], land_recv.at[way],
            ))
        return copies

    def pass_copies(way):
        copies = []
        for f, far in land_rows:
            _, at = edge(way, 1, far)
            copies.append(pltpu.make_async_remote_copy(
                src_ref=S.at[f, at, parity], dst_ref=S.at[f, at, parity],
                send_sem=tile_send.at[1 - way], recv_sem=pass_recv.at[way],
                device_id={"sub": mate}, device_id_type=pl.DeviceIdType.MESH,
            ))
        return copies

    def halo_copies(way, g):
        near, far = (REACHES[g - 1] if g > 0 else 0) + 1, REACHES[g]
        parts = [(pl.ds(0, 3), near, far)]
        if g == groups - 1:
            parts = [(pl.ds(0, 3), near, far - 1), (pl.ds(1, 1), far, far)]
        copies = []
        for fields, first, last in parts:
            source, target = edge(way, first, last)
            copies.append(to_tile(
                way, S.at[fields, source], S.at[fields, target],
                tile_send.at[way], halo_recv.at[way, g],
            ))
        return copies

    def halo_bytes(g):
        count = REACHES[g] - (REACHES[g - 1] if g > 0 else 0)
        return S.at[0, pl.ds(0, 3 * count - (2 if g == groups - 1 else 0))]

    def wait_for(some, sem):
        pltpu.make_async_copy(some, some, sem).wait()

    comes = (has_up, has_down)
    goes = (has_down, has_up)

    def enter():
        pl.semaphore_wait(
            barrier, pairs + has_up.astype(jnp.int32) + has_down.astype(jnp.int32)
        )
    def send_land():
        for way in range(2):

            @pl.when(goes[way])
            def _():
                for copy in land_copies(way):
                    copy.start()

    def send_halo(g):
        for way in range(2):

            @pl.when(goes[way])
            def _():
                for copy in halo_copies(way, g):
                    copy.start()

    def pass_land():
        for way in range(2):

            @pl.when(comes[way])
            def _():
                wait_for(land_bytes, land_recv.at[way])
                for copy in pass_copies(way):
                    copy.start()

    def take_land():
        for way in range(2):

            @pl.when(comes[way])
            def _():
                wait_for(land_bytes, pass_recv.at[way])

    def take_halo(g):
        for way in range(2):

            @pl.when(comes[way])
            def _():
                wait_for(halo_bytes(g), halo_recv.at[way, g])

    lane = lax.broadcasted_iota(jnp.int32, (1, half, LANES), 2)
    is_first, is_last = lane == 0, lane == LANES - 1

    def get(ref, lead, start, count):
        at = pl.ds(HALO + start, count)
        return ref[lead + (at, 0)], ref[lead + (at, 1)]

    def put(ref, lead, start, count, value):
        at = pl.ds(HALO + start, count)
        ref[lead + (at, 0)] = value[0]
        ref[lead + (at, 1)] = value[1]

    def each(function, *values):
        return tuple(function(*parts) for parts in zip(*values))

    def sides(value):
        even, odd = value
        even_up, odd_up = pltpu.roll(even, LANES - 1, 2), pltpu.roll(odd, LANES - 1, 2)
        even_down, odd_down = pltpu.roll(even, 1, 2), pltpu.roll(odd, 1, 2)
        following = (
            jnp.where(is_last, odd_up, even_up),
            jnp.where(is_last, pltpu.roll(even_up, half - 1, 1), odd_up),
        )
        previous = (
            jnp.where(is_first, pltpu.roll(odd_down, 1, 1), even_down),
            jnp.where(is_first, even_down, odd_down),
        )
        return following, previous

    def col_diff(value):
        following, previous = sides(value)
        return each(lambda a, b: a - b, following, previous)

    def row_diff(value):
        return each(lambda a: a[2:] - a[:-2], value)

    def inner_rows(value):
        return each(lambda a: a[1:-1], value)

    up_scale = jnp.where(has_up, 1.0, 0.0)
    down_scale = jnp.where(has_down, 1.0, 0.0)

    def masked(value, start, count):
        if not isinstance(start, int) or (start >= 0 and start + count <= rows):
            return value
        scales = []
        for r in range(start, start + count):
            scales.append(up_scale if r < 0 else down_scale if r >= rows else None)

        def scale(part):
            return jnp.concatenate(
                [part[i:i + 1] if s is None else part[i:i + 1] * s for i, s in enumerate(scales)], 0
            )

        return each(scale, value)

    def field(step, f):
        return (S, (f,)) if step == 0 else (E, (step - 1, f))

    def height_stage(step, start, count):
        h_ref, h_at = field(step, 0)
        u_ref, u_at = field(step, 1)
        v_ref, v_at = field(step, 2)
        wide_d = get(S, (DEPTH,), start - 1, count + 2)
        flux_x = each(jnp.multiply, wide_d, get(u_ref, u_at, start - 1, count + 2))
        flux_y = each(jnp.multiply, inner_rows(wide_d), get(v_ref, v_at, start, count))
        h = get(h_ref, h_at, start, count)
        new_h = each(
            lambda a, x, y: a - (time_step * 0.5) * (x + y), h, row_diff(flux_x), col_diff(flux_y)
        )
        put(E, (step, 0), start, count, masked(new_h, start, count))

    def wind_stage(step, start, count):
        u_ref, u_at = field(step, 1)
        v_ref, v_at = field(step, 2)
        wide_h = get(E, (step, 0), start - 1, count + 2)
        u = get(u_ref, u_at, start, count)
        v = get(v_ref, v_at, start, count)
        pull, turn = time_step * gravity * 0.5, time_step * coriolis
        new_u = each(lambda a, b, x: a - pull * x + turn * b, u, v, row_diff(wide_h))
        new_v = each(lambda a, b, y: b - pull * y - turn * a, u, v, col_diff(inner_rows(wide_h)))
        if step == FSTEPS - 1:
            new_u, new_v = masked(new_u, start, count), masked(new_v, start, count)
        put(E, (step, 1), start, count, new_u)
        put(E, (step, 2), start, count, new_v)

    def spread(ref, at, start, count, kappa, rest):
        wide = get(ref, at, start - 1, count + 2)
        w = inner_rows(wide)
        following, previous = sides(w)
        return each(
            lambda a, n, p, c, k, r: r * c + k * ((a[2:] + a[:-2]) + (n + p)),
            wide, following, previous, w, kappa, rest,
        )

    def coefficients(start, count):
        kappa = get(S, (KAPPA,), start, count)
        return kappa, each(lambda k: 1.0 - 4.0 * k, kappa)

    def spread_stage(step, start, count):
        kappa, rest = coefficients(start, count)
        for f in range(6):
            if step == 0:
                ref, at = field(FSTEPS, f - 3) if f >= 3 else field(0, f)
            else:
                ref, at = W, (step - 1, f)
            put(W, (step, f), start, count, spread(ref, at, start, count, kappa, rest))

    stages = []
    for step in range(FSTEPS):
        stages.append((functools.partial(height_stage, step), HALO - 1 - 2 * step, 4))
        stages.append((functools.partial(wind_stage, step), HALO - 2 - 2 * step, 4))
    for step in range(DSTEPS):
        stages.append((functools.partial(spread_stage, step), DSTEPS - 1 - step, 4))

    def advance(stage, lo, hi, size):
        count = hi - lo
        whole = count // size
        if whole > 1:

            def body(i, carry):
                stage(lo + i * size, size)
                return carry

            for i in range(whole):
                body(i, 0)
            lo += whole * size
        elif whole == 1:
            stage(lo, size)
            lo += size
        if hi > lo:
            stage(lo, hi - lo)

    def compute(g, chosen=stages):
        for stage, margin, size in chosen:
            for lo, count, _ in pieces[g]:
                hi = lo + count
                if g == 0:
                    advance(stage, lo - margin, hi + margin, size)
                elif hi <= windows[0][0]:
                    advance(stage, lo - margin, hi - margin, size)
                else:
                    advance(stage, lo + margin, hi + margin, size)

    moves, spreads = stages[:2 * FSTEPS], stages[2 * FSTEPS:]

    def spread_inner():
        lo, hi = windows[1]
        for stage, margin, size in spreads:
            advance(stage, lo - margin, hi + margin, size)

    later = jnp.minimum(me + 1, subs - 1)
    keep = jnp.where(me < subs - 1, 1.0, 0.0)

    def weights(s):
        return mixing[s, me], mixing[s, later] * keep

    dest_pair = [lax.rem(pair + k, pairs) for k in range(pairs)]
    w_mine = [weights(q * 2 + parity) for q in dest_pair]
    w_mate = [weights(q * 2 + 1 - parity) for q in dest_pair]
    order = list(range(1, pairs)) + [0]

    def span(g):
        first = pieces[g][0][2]
        return pl.ds(first, sum(count for _, count, _ in pieces[g]))

    def a_copy(g, k):
        at = (k, slice(None), span(g))
        return pltpu.make_async_remote_copy(
            src_ref=send_a.at[at], dst_ref=recv_a.at[at],
            send_sem=a_send, recv_sem=a_recv.at[g, k],
            device_id={"sub": mate}, device_id_type=pl.DeviceIdType.MESH,
        )

    def b_copy(g, k):
        at = (k - 1, slice(None), span(g))
        return pltpu.make_async_remote_copy(
            src_ref=send_b.at[at], dst_ref=recv_b.at[at],
            send_sem=b_send, recv_sem=b_recv.at[g, k - 1],
            device_id={"sub": dest_pair[k] * 2 + parity},
            device_id_type=pl.DeviceIdType.MESH,
        )

    def mix_first(weight, ref, k):
        (lo, count, place), = pieces[0]
        a, b = weight

        def mix(start, n):
            for f in range(3):
                ref_end, at_end = field(FSTEPS, f)
                ends = get(ref_end, at_end, start, n)
                put(Z, (0, f), start, n, each(lambda x, y: a * x - b * y, get(S, (f,), start, n), ends))

        def spread_mixed(step, start, n):
            kappa, rest = coefficients(start, n)
            for f in range(3):
                new = spread(Z, (step, f), start, n, kappa, rest)
                if step < DSTEPS - 1:
                    put(Z, (step + 1, f), start, n, new)
                else:
                    for e in range(2):
                        ref[k, f, pl.ds(place + start - lo, n), e] = new[e]

        advance(mix, lo - DSTEPS, lo + count + DSTEPS, 4)
        for step in range(DSTEPS):
            margin = DSTEPS - 1 - step
            advance(functools.partial(spread_mixed, step), lo - margin, lo + count + margin, 4)

    def mate_terms(g, k):
        for lo, count, place in pieces[g]:
            at = pl.ds(place, count)
            for f in range(3):
                start = W[DSTEPS - 1, f, pl.ds(HALO + lo, count)]
                end = W[DSTEPS - 1, 3 + f, pl.ds(HALO + lo, count)]
                a, b = w_mate[k]
                send_a[k, f, at] = a * start - b * end
        a_copy(g, k).start()

    def own_terms(g, k):
        for lo, count, place in pieces[g]:
            at = pl.ds(place, count)
            for f in range(3):
                start = W[DSTEPS - 1, f, pl.ds(HALO + lo, count)]
                end = W[DSTEPS - 1, 3 + f, pl.ds(HALO + lo, count)]
                a, b = w_mine[k]
                mine = a * start - b * end
                if k == 0:
                    M[f, at] = mine
                else:
                    send_b[k - 1, f, at] = mine

    def terms(g):
        for k in order:
            mate_terms(g, k)
        for k in order:
            own_terms(g, k)

    def join(g):
        for k in range(1, pairs):
            a_copy(g, k).wait_recv()
            at = (k - 1, slice(None), span(g))
            send_b[at] = send_b[at] + recv_a[(k, slice(None), span(g))]
            b_copy(g, k).start()

    def finish(g):
        a_copy(g, 0).wait_recv()
        for k in range(1, pairs):
            b_copy(g, k).wait_recv()
        for lo, count, place in pieces[g]:
            for f in range(3):
                for i in range(count):
                    r = lo + i
                    total = M[f, place + i] + recv_a[0, f, place + i]
                    for k in range(1, pairs):
                        total = total + recv_b[k - 1, f, place + i]
                    base = (f * (rows // SUBLANES) + r // SUBLANES) * blocks * SUBLANES + r % SUBLANES
                    for e in range(2):
                        out[pl.ds(base + e * SUBLANES, half, stride=2 * SUBLANES), :] = total[e]

    enter()
    send_land()
    send_halo(0)
    if pairs == 2:
        compute(0, moves)
        mix_first(w_mate[1], send_a, 1)
        a_copy(0, 1).start()
        send_halo(1)
        mix_first(w_mine[1], send_b, 0)
        join(0)
        compute(1, moves)
        spread_inner()
        terms(1)
    else:
        compute(0)
        terms(0)
        join(0)
        send_halo(1)
        compute(1)
        terms(1)
    pass_land()
    for g in range(2, groups):
        send_halo(g)
    join(1)
    if pairs == 2:
        mate_terms(0, 0)
        own_terms(0, 0)
    take_land()
    for g in range(groups):
        take_halo(g)
        compute(g + 2)
        terms(g + 2)
        join(g + 2)
    for g in range(groups + 2):
        finish(g)

    pltpu.make_async_copy(send_a, send_a, a_send).wait()
    if pairs > 1:
        pltpu.make_async_copy(send_b, send_b, b_send).wait()
    sent = S.at[0, pl.ds(0, 3 * HALO - 2 + HALO + DSTEPS - 1)]
    for way in range(2):

        @pl.when(goes[way])
        def _():
            wait_for(sent, tile_send.at[way])


def solution(mesh):
    subs, tiles = mesh.shape["sub"], mesh.shape["tile"]

    def local(states, terrain, depth_table, spread_table, mixing):
        _, fields, rows, cols = states.shape
        pairs = subs // 2
        many = max(pairs - 1, 1)
        blocks = cols // LANES
        row = (2, blocks // 2, LANES)
        tall = rows + 2 * HALO
        dma = pltpu.SemaphoreType.DMA
        phases = len(windows_of(rows))
        vmem = pltpu.VMEM

        def flat(value):
            tiles_last = value.reshape(rows // SUBLANES, SUBLANES, blocks, LANES)
            return tiles_last.transpose(0, 2, 1, 3).reshape(-1, LANES)

        result = pl.pallas_call(
            functools.partial(kernel, subs, tiles, rows, cols, depth_table.shape[0]),
            out_shape=jax.ShapeDtypeStruct((fields * rows * blocks, LANES), jnp.float32),
            in_specs=[pl.BlockSpec(memory_space=pltpu.HBM)] * 5,
            out_specs=pl.BlockSpec(memory_space=pltpu.VMEM),
            scratch_shapes=[
                pltpu.SMEM(depth_table.shape, jnp.float32),
                pltpu.SMEM(spread_table.shape, jnp.float32),
                pltpu.SMEM(mixing.shape, jnp.float32),
                vmem((rows * blocks, LANES), jnp.int32),
                vmem((5, tall) + row, jnp.float32),
                vmem((FSTEPS, fields, tall) + row, jnp.float32),
                vmem((DSTEPS, 2 * fields, tall) + row, jnp.float32),
                vmem((DSTEPS, fields, tall) + row, jnp.float32),
                vmem((pairs, fields, rows) + row, jnp.float32),
                vmem((pairs, fields, rows) + row, jnp.float32),
                vmem((many, fields, rows) + row, jnp.float32),
                vmem((many, fields, rows) + row, jnp.float32),
                vmem((fields, rows) + row, jnp.float32),
                dma((5,)),
                dma((2,)),
                dma((2,)),
                dma((2,)),
                dma((2, len(REACHES))),
                dma(()),
                dma((phases, pairs)),
                dma(()),
                dma((phases, many)),
            ],
            compiler_params=pltpu.CompilerParams(
                collective_id=0, has_side_effects=True, vmem_limit_bytes=46 * 1024 * 1024
            ),
            name="gradient",
        )(
            *(
                pltpu.with_memory_space_constraint(value, pltpu.HBM)
                for value in (depth_table, spread_table, mixing, states, flat(terrain))
            )
        )
        tiled = result.reshape(fields, rows // SUBLANES, blocks, SUBLANES, LANES)
        return tiled.transpose(0, 1, 3, 2, 4).reshape(states.shape)

    in_specs = (P("sub", None, "tile", None), P("tile", None), P(), P(), P())
    out_specs = P("sub", None, "tile", None)
    return jax.shard_map(local, mesh=mesh, in_specs=in_specs, out_specs=out_specs, check_vma=False)
```

```python
import functools

import jax
import jax.numpy as jnp
from jax import lax
from jax.experimental import pallas as pl
from jax.experimental.pallas import tpu as pltpu
from jax.sharding import PartitionSpec as P

FSTEPS = 3
DSTEPS = 3
time_step = 0.5
gravity = 1.0
coriolis = 0.3

LANES = 128
SUBLANES = 8
HALO = 2 * FSTEPS + DSTEPS
REACHES = (2, 4, 7, 9)
DEPTH, KAPPA = 3, 4


def windows_of(rows):
    middle = rows // 2
    found = [(HALO, middle), (HALO, rows - HALO)]
    for reach in REACHES:
        found.append((HALO - reach, rows - HALO + reach))
    return found


def pieces_of(rows):
    last, place, pieces = None, 0, []
    for window in windows_of(rows):
        spans = [window] if last is None else [(window[0], last[0]), (last[1], window[1])]
        last = window
        held = []
        for lo, hi in spans:
            if hi > lo:
                held.append((lo, hi - lo, place))
                place += hi - lo
        pieces.append(held)
    return pieces


def kernel(
    subs, tiles, rows, cols, nclass,
    depth_in, spread_in, mixing_in, states, terrain, out,
    depth_tab, spread_tab, mixing, T, S, E, W, Z, send_a, recv_a, send_b, recv_b, M,
    load_sem, tile_send, land_recv, pass_recv, halo_recv, a_send, a_recv, b_send, b_recv,
):
    pairs = subs // 2
    blocks = cols // LANES
    half = blocks // 2
    me = lax.axis_index("sub")
    tile = lax.axis_index("tile")
    parity = lax.rem(me, 2)
    mate = me + 1 - 2 * parity
    pair = me // 2
    has_up = tile > 0
    has_down = tile < tiles - 1
    up, down = tile - 1, tile + 1
    windows, pieces = windows_of(rows), pieces_of(rows)
    groups = len(REACHES)

    tables = [
        pltpu.make_async_copy(depth_in, depth_tab, load_sem.at[2]),
        pltpu.make_async_copy(spread_in, spread_tab, load_sem.at[3]),
        pltpu.make_async_copy(mixing_in, mixing, load_sem.at[4]),
    ]
    own = pl.ds(HALO, rows)
    pltpu.make_async_copy(terrain, T, load_sem.at[0]).start()
    for copy in tables:
        copy.start()
    for b in range(blocks):
        at = pl.ds(b * LANES, LANES)
        pltpu.make_async_copy(
            states.at[0, :, :, at], S.at[pl.ds(0, 3), own, b % 2, b // 2], load_sem.at[1]
        ).start()

    barrier = pltpu.get_barrier_semaphore()
    pl.semaphore_signal(barrier, inc=1, device_id={"sub": mate})
    for k in range(1, pairs):
        pl.semaphore_signal(
            barrier, inc=1, device_id={"sub": lax.rem(pair + k, pairs) * 2 + parity}
        )

    @pl.when(has_up)
    def _():
        pl.semaphore_signal(barrier, inc=1, device_id={"tile": up})

    @pl.when(has_down)
    def _():
        pl.semaphore_signal(barrier, inc=1, device_id={"tile": down})

    @pl.when(jnp.logical_not(has_up))
    def _():
        S[:, 0:HALO] = jnp.zeros((5, HALO, 2, half, LANES), jnp.float32)

    @pl.when(jnp.logical_not(has_down))
    def _():
        S[:, HALO + rows:] = jnp.zeros((5, HALO, 2, half, LANES), jnp.float32)

    pltpu.make_async_copy(T, T, load_sem.at[0]).wait()
    for copy in tables:
        copy.wait()
    def lookup(i, carry):
        for j in range(SUBLANES):
            for e in range(2):
                first = (i * blocks + e) * SUBLANES + j
                kind = T[pl.ds(first, half, stride=2 * SUBLANES), :]
                depth = jnp.zeros(kind.shape, jnp.float32)
                kappa = jnp.zeros(kind.shape, jnp.float32)
                for n in range(nclass):
                    hit = kind == n
                    depth = jnp.where(hit, depth_tab[n], depth)
                    kappa = jnp.where(hit, spread_tab[n], kappa)
                S[DEPTH, HALO + i * SUBLANES + j, e] = depth
                S[KAPPA, HALO + i * SUBLANES + j, e] = kappa
        return carry

    lax.fori_loop(0, rows // SUBLANES, lookup, 0)
    loaded = S.at[pl.ds(0, 3), own]
    pltpu.make_async_copy(loaded, loaded, load_sem.at[1]).wait()

    def edge(way, near, far):
        count = far - near + 1
        if way == 0:
            return pl.ds(HALO + rows - far, count), pl.ds(HALO - far, count)
        return pl.ds(HALO + near - 1, count), pl.ds(HALO + rows + near - 1, count)

    def to_tile(way, source, target, send, recv):
        return pltpu.make_async_remote_copy(
            src_ref=source, dst_ref=target, send_sem=send, recv_sem=recv,
            device_id={"tile": down if way == 0 else up}, device_id_type=pl.DeviceIdType.MESH,
        )

    land_rows = ((DEPTH, HALO), (KAPPA, DSTEPS - 1))
    land_bytes = S.at[0, pl.ds(0, HALO + DSTEPS - 1), 0]

    def land_copies(way):
        copies = []
        for f, far in land_rows:
            source, target = edge(way, 1, far)
            copies.append(to_tile(
                way, S.at[f, source, parity], S.at[f, target, parity],
                tile_send.at[way], land_recv.at[way],
            ))
        return copies

    def pass_copies(way):
        copies = []
        for f, far in land_rows:
            _, at = edge(way, 1, far)
            copies.append(pltpu.make_async_remote_copy(
                src_ref=S.at[f, at, parity], dst_ref=S.at[f, at, parity],
                send_sem=tile_send.at[1 - way], recv_sem=pass_recv.at[way],
                device_id={"sub": mate}, device_id_type=pl.DeviceIdType.MESH,
            ))
        return copies

    def halo_copies(way, g):
        near, far = (REACHES[g - 1] if g > 0 else 0) + 1, REACHES[g]
        parts = [(pl.ds(0, 3), near, far)]
        if g == groups - 1:
            parts = [(pl.ds(0, 3), near, far - 1), (pl.ds(1, 1), far, far)]
        copies = []
        for fields, first, last in parts:
            source, target = edge(way, first, last)
            copies.append(to_tile(
                way, S.at[fields, source], S.at[fields, target],
                tile_send.at[way], halo_recv.at[way, g],
            ))
        return copies

    def halo_bytes(g):
        count = REACHES[g] - (REACHES[g - 1] if g > 0 else 0)
        return S.at[0, pl.ds(0, 3 * count - (2 if g == groups - 1 else 0))]

    def wait_for(some, sem):
        pltpu.make_async_copy(some, some, sem).wait()

    comes = (has_up, has_down)
    goes = (has_down, has_up)

    def enter():
        pl.semaphore_wait(
            barrier, pairs + has_up.astype(jnp.int32) + has_down.astype(jnp.int32)
        )
    def send_land():
        for way in range(2):

            @pl.when(goes[way])
            def _():
                for copy in land_copies(way):
                    copy.start()

    def send_halo(g):
        for way in range(2):

            @pl.when(goes[way])
            def _():
                for copy in halo_copies(way, g):
                    copy.start()

    def pass_land():
        for way in range(2):

            @pl.when(comes[way])
            def _():
                wait_for(land_bytes, land_recv.at[way])
                for copy in pass_copies(way):
                    copy.start()

    def take_land():
        for way in range(2):

            @pl.when(comes[way])
            def _():
                wait_for(land_bytes, pass_recv.at[way])

    def take_halo(g):
        for way in range(2):

            @pl.when(comes[way])
            def _():
                wait_for(halo_bytes(g), halo_recv.at[way, g])

    lane = lax.broadcasted_iota(jnp.int32, (1, half, LANES), 2)
    is_first, is_last = lane == 0, lane == LANES - 1

    def get(ref, lead, start, count):
        at = pl.ds(HALO + start, count)
        return ref[lead + (at, 0)], ref[lead + (at, 1)]

    def put(ref, lead, start, count, value):
        at = pl.ds(HALO + start, count)
        ref[lead + (at, 0)] = value[0]
        ref[lead + (at, 1)] = value[1]

    def each(function, *values):
        return tuple(function(*parts) for parts in zip(*values))

    def sides(value):
        even, odd = value
        even_up, odd_up = pltpu.roll(even, LANES - 1, 2), pltpu.roll(odd, LANES - 1, 2)
        even_down, odd_down = pltpu.roll(even, 1, 2), pltpu.roll(odd, 1, 2)
        following = (
            jnp.where(is_last, odd_up, even_up),
            jnp.where(is_last, pltpu.roll(even_up, half - 1, 1), odd_up),
        )
        previous = (
            jnp.where(is_first, pltpu.roll(odd_down, 1, 1), even_down),
            jnp.where(is_first, even_down, odd_down),
        )
        return following, previous

    def col_diff(value):
        following, previous = sides(value)
        return each(lambda a, b: a - b, following, previous)

    def row_diff(value):
        return each(lambda a: a[2:] - a[:-2], value)

    def inner_rows(value):
        return each(lambda a: a[1:-1], value)

    up_scale = jnp.where(has_up, 1.0, 0.0)
    down_scale = jnp.where(has_down, 1.0, 0.0)

    def masked(value, start, count):
        if not isinstance(start, int) or (start >= 0 and start + count <= rows):
            return value
        scales = []
        for r in range(start, start + count):
            scales.append(up_scale if r < 0 else down_scale if r >= rows else None)

        def scale(part):
            return jnp.concatenate(
                [part[i:i + 1] if s is None else part[i:i + 1] * s for i, s in enumerate(scales)], 0
            )

        return each(scale, value)

    def field(step, f):
        return (S, (f,)) if step == 0 else (E, (step - 1, f))

    def height_stage(step, start, count):
        h_ref, h_at = field(step, 0)
        u_ref, u_at = field(step, 1)
        v_ref, v_at = field(step, 2)
        wide_d = get(S, (DEPTH,), start - 1, count + 2)
        flux_x = each(jnp.multiply, wide_d, get(u_ref, u_at, start - 1, count + 2))
        flux_y = each(jnp.multiply, inner_rows(wide_d), get(v_ref, v_at, start, count))
        h = get(h_ref, h_at, start, count)
        new_h = each(
            lambda a, x, y: a - (time_step * 0.5) * (x + y), h, row_diff(flux_x), col_diff(flux_y)
        )
        put(E, (step, 0), start, count, masked(new_h, start, count))

    def wind_stage(step, start, count):
        u_ref, u_at = field(step, 1)
        v_ref, v_at = field(step, 2)
        wide_h = get(E, (step, 0), start - 1, count + 2)
        u = get(u_ref, u_at, start, count)
        v = get(v_ref, v_at, start, count)
        pull, turn = time_step * gravity * 0.5, time_step * coriolis
        new_u = each(lambda a, b, x: a - pull * x + turn * b, u, v, row_diff(wide_h))
        new_v = each(lambda a, b, y: b - pull * y - turn * a, u, v, col_diff(inner_rows(wide_h)))
        if step == FSTEPS - 1:
            new_u, new_v = masked(new_u, start, count), masked(new_v, start, count)
        put(E, (step, 1), start, count, new_u)
        put(E, (step, 2), start, count, new_v)

    def spread(ref, at, start, count, kappa, rest):
        wide = get(ref, at, start - 1, count + 2)
        w = inner_rows(wide)
        following, previous = sides(w)
        return each(
            lambda a, n, p, c, k, r: r * c + k * ((a[2:] + a[:-2]) + (n + p)),
            wide, following, previous, w, kappa, rest,
        )

    def coefficients(start, count):
        kappa = get(S, (KAPPA,), start, count)
        return kappa, each(lambda k: 1.0 - 4.0 * k, kappa)

    def spread_stage(step, start, count):
        kappa, rest = coefficients(start, count)
        for f in range(6):
            if step == 0:
                ref, at = field(FSTEPS, f - 3) if f >= 3 else field(0, f)
            else:
                ref, at = W, (step - 1, f)
            put(W, (step, f), start, count, spread(ref, at, start, count, kappa, rest))

    stages = []
    for step in range(FSTEPS):
        stages.append((functools.partial(height_stage, step), HALO - 1 - 2 * step, 4))
        stages.append((functools.partial(wind_stage, step), HALO - 2 - 2 * step, 4))
    for step in range(DSTEPS):
        stages.append((functools.partial(spread_stage, step), DSTEPS - 1 - step, 4))

    def advance(stage, lo, hi, size):
        count = hi - lo
        whole = count // size
        if whole > 1:

            def body(i, carry):
                stage(lo + i * size, size)
                return carry

            for i in range(whole):
                body(i, 0)
            lo += whole * size
        elif whole == 1:
            stage(lo, size)
            lo += size
        if hi > lo:
            stage(lo, hi - lo)

    def compute(g, chosen=stages):
        for stage, margin, size in chosen:
            for lo, count, _ in pieces[g]:
                hi = lo + count
                if g == 0:
                    advance(stage, lo - margin, hi + margin, size)
                elif hi <= windows[0][0]:
                    advance(stage, lo - margin, hi - margin, size)
                else:
                    advance(stage, lo + margin, hi + margin, size)

    moves, spreads = stages[:2 * FSTEPS], stages[2 * FSTEPS:]

    def spread_inner():
        lo, hi = windows[1]
        for stage, margin, size in spreads:
            advance(stage, lo - margin, hi + margin, size)

    later = jnp.minimum(me + 1, subs - 1)
    keep = jnp.where(me < subs - 1, 1.0, 0.0)

    def weights(s):
        return mixing[s, me], mixing[s, later] * keep

    dest_pair = [lax.rem(pair + k, pairs) for k in range(pairs)]
    w_mine = [weights(q * 2 + parity) for q in dest_pair]
    w_mate = [weights(q * 2 + 1 - parity) for q in dest_pair]
    order = list(range(1, pairs)) + [0]

    def span(g):
        first = pieces[g][0][2]
        return pl.ds(first, sum(count for _, count, _ in pieces[g]))

    def a_copy(g, k):
        at = (k, slice(None), span(g))
        return pltpu.make_async_remote_copy(
            src_ref=send_a.at[at], dst_ref=recv_a.at[at],
            send_sem=a_send, recv_sem=a_recv.at[g * (pairs - 1) + k if k > 0 else 0],
            device_id={"sub": mate}, device_id_type=pl.DeviceIdType.MESH,
        )

    def b_copy(g, k):
        at = (k - 1, slice(None), span(g))
        return pltpu.make_async_remote_copy(
            src_ref=send_b.at[at], dst_ref=recv_b.at[at],
            send_sem=b_send, recv_sem=b_recv.at[g, k - 1],
            device_id={"sub": dest_pair[k] * 2 + parity},
            device_id_type=pl.DeviceIdType.MESH,
        )

    def mix_first(weight, ref, k):
        (lo, count, place), = pieces[0]
        a, b = weight

        def mix(start, n):
            for f in range(3):
                ref_end, at_end = field(FSTEPS, f)
                ends = get(ref_end, at_end, start, n)
                put(Z, (0, f), start, n, each(lambda x, y: a * x - b * y, get(S, (f,), start, n), ends))

        def spread_mixed(step, start, n):
            kappa, rest = coefficients(start, n)
            for f in range(3):
                new = spread(Z, (step, f), start, n, kappa, rest)
                if step < DSTEPS - 1:
                    put(Z, (step + 1, f), start, n, new)
                else:
                    for e in range(2):
                        ref[k, f, pl.ds(place + start - lo, n), e] = new[e]

        advance(mix, lo - DSTEPS, lo + count + DSTEPS, 4)
        for step in range(DSTEPS):
            margin = DSTEPS - 1 - step
            advance(functools.partial(spread_mixed, step), lo - margin, lo + count + margin, 4)

    def mate_terms(g, k):
        for lo, count, place in pieces[g]:
            at = pl.ds(place, count)
            for f in range(3):
                start = W[DSTEPS - 1, f, pl.ds(HALO + lo, count)]
                end = W[DSTEPS - 1, 3 + f, pl.ds(HALO + lo, count)]
                a, b = w_mate[k]
                send_a[k, f, at] = a * start - b * end
        a_copy(g, k).start()

    def own_terms(g, k):
        for lo, count, place in pieces[g]:
            at = pl.ds(place, count)
            for f in range(3):
                start = W[DSTEPS - 1, f, pl.ds(HALO + lo, count)]
                end = W[DSTEPS - 1, 3 + f, pl.ds(HALO + lo, count)]
                a, b = w_mine[k]
                mine = a * start - b * end
                if k == 0:
                    M[f, at] = mine
                else:
                    send_b[k - 1, f, at] = mine

    def terms(g):
        for k in order:
            mate_terms(g, k)
        for k in order:
            own_terms(g, k)

    def join(g):
        for k in range(1, pairs):
            a_copy(g, k).wait_recv()
            at = (k - 1, slice(None), span(g))
            send_b[at] = send_b[at] + recv_a[(k, slice(None), span(g))]
            b_copy(g, k).start()

    def finish(g):
        for k in range(1, pairs):
            b_copy(g, k).wait_recv()
        for lo, count, place in pieces[g]:
            for f in range(3):
                for i in range(count):
                    r = lo + i
                    total = M[f, place + i] + recv_a[0, f, place + i]
                    for k in range(1, pairs):
                        total = total + recv_b[k - 1, f, place + i]
                    base = (f * (rows // SUBLANES) + r // SUBLANES) * blocks * SUBLANES + r % SUBLANES
                    for e in range(2):
                        out[pl.ds(base + e * SUBLANES, half, stride=2 * SUBLANES), :] = total[e]

    enter()
    send_land()
    send_halo(0)
    if pairs == 2:
        compute(0, moves)
        mix_first(w_mate[1], send_a, 1)
        a_copy(0, 1).start()
        send_halo(1)
        mix_first(w_mine[1], send_b, 0)
        join(0)
        compute(1, moves)
        spread_inner()
        terms(1)
    else:
        compute(0)
        terms(0)
        join(0)
        send_halo(1)
        compute(1)
        terms(1)
    pass_land()
    for g in range(2, groups):
        send_halo(g)
    join(1)
    if pairs == 2:
        mate_terms(0, 0)
        own_terms(0, 0)
    take_land()
    for g in range(groups):
        take_halo(g)
        compute(g + 2)
        terms(g + 2)
        join(g + 2)
    wait_for(recv_a.at[0], a_recv.at[0])
    for g in range(groups + 2):
        finish(g)

    pltpu.make_async_copy(send_a, send_a, a_send).wait()
    if pairs > 1:
        pltpu.make_async_copy(send_b, send_b, b_send).wait()
    sent = S.at[0, pl.ds(0, 3 * HALO - 2 + HALO + DSTEPS - 1)]
    for way in range(2):

        @pl.when(goes[way])
        def _():
            wait_for(sent, tile_send.at[way])


def solution(mesh):
    subs, tiles = mesh.shape["sub"], mesh.shape["tile"]

    def local(states, terrain, depth_table, spread_table, mixing):
        _, fields, rows, cols = states.shape
        pairs = subs // 2
        many = max(pairs - 1, 1)
        blocks = cols // LANES
        row = (2, blocks // 2, LANES)
        tall = rows + 2 * HALO
        dma = pltpu.SemaphoreType.DMA
        phases = len(windows_of(rows))
        vmem = pltpu.VMEM

        def flat(value):
            tiles_last = value.reshape(rows // SUBLANES, SUBLANES, blocks, LANES)
            return tiles_last.transpose(0, 2, 1, 3).reshape(-1, LANES)

        result = pl.pallas_call(
            functools.partial(kernel, subs, tiles, rows, cols, depth_table.shape[0]),
            out_shape=jax.ShapeDtypeStruct((fields * rows * blocks, LANES), jnp.float32),
            in_specs=[pl.BlockSpec(memory_space=pltpu.HBM)] * 5,
            out_specs=pl.BlockSpec(memory_space=pltpu.VMEM),
            scratch_shapes=[
                pltpu.SMEM(depth_table.shape, jnp.float32),
                pltpu.SMEM(spread_table.shape, jnp.float32),
                pltpu.SMEM(mixing.shape, jnp.float32),
                vmem((rows * blocks, LANES), jnp.int32),
                vmem((5, tall) + row, jnp.float32),
                vmem((FSTEPS, fields, tall) + row, jnp.float32),
                vmem((DSTEPS, 2 * fields, tall) + row, jnp.float32),
                vmem((DSTEPS, fields, tall) + row, jnp.float32),
                vmem((pairs, fields, rows) + row, jnp.float32),
                vmem((pairs, fields, rows) + row, jnp.float32),
                vmem((many, fields, rows) + row, jnp.float32),
                vmem((many, fields, rows) + row, jnp.float32),
                vmem((fields, rows) + row, jnp.float32),
                dma((5,)),
                dma((2,)),
                dma((2,)),
                dma((2,)),
                dma((2, len(REACHES))),
                dma(()),
                dma((phases * (pairs - 1) + 1,)),
                dma(()),
                dma((phases, many)),
            ],
            compiler_params=pltpu.CompilerParams(
                collective_id=0, has_side_effects=True, vmem_limit_bytes=46 * 1024 * 1024
            ),
            name="gradient",
        )(
            *(
                pltpu.with_memory_space_constraint(value, pltpu.HBM)
                for value in (depth_table, spread_table, mixing, states, flat(terrain))
            )
        )
        tiled = result.reshape(fields, rows // SUBLANES, blocks, SUBLANES, LANES)
        return tiled.transpose(0, 1, 3, 2, 4).reshape(states.shape)

    in_specs = (P("sub", None, "tile", None), P("tile", None), P(), P(), P())
    out_specs = P("sub", None, "tile", None)
    return jax.shard_map(local, mesh=mesh, in_specs=in_specs, out_specs=out_specs, check_vma=False)
```

```python
import functools

import jax
import jax.numpy as jnp
from jax import lax
from jax.experimental import pallas as pl
from jax.experimental.pallas import tpu as pltpu
from jax.sharding import PartitionSpec as P

FSTEPS = 3
DSTEPS = 3
time_step = 0.5
gravity = 1.0
coriolis = 0.3

LANES = 128
SUBLANES = 8
HALO = 2 * FSTEPS + DSTEPS
REACHES = (2, 4, 7, 9)
DEPTH, KAPPA = 3, 4


def windows_of(rows):
    middle = rows // 2
    found = [(HALO, middle), (HALO, rows - HALO)]
    for reach in REACHES:
        found.append((HALO - reach, rows - HALO + reach))
    return found


def pieces_of(rows):
    last, place, pieces = None, 0, []
    for window in windows_of(rows):
        spans = [window] if last is None else [(window[0], last[0]), (last[1], window[1])]
        last = window
        held = []
        for lo, hi in spans:
            if hi > lo:
                held.append((lo, hi - lo, place))
                place += hi - lo
        pieces.append(held)
    return pieces


def kernel(
    subs, tiles, rows, cols, nclass,
    depth_in, spread_in, mixing_in, states, terrain, out,
    depth_tab, spread_tab, mixing, T, S, E, W, Z, send_a, recv_a, send_b, recv_b, M,
    load_sem, tile_send, land_recv, pass_recv, halo_recv, a_send, a_recv, b_send, b_recv,
):
    pairs = subs // 2
    blocks = cols // LANES
    half = blocks // 2
    me = lax.axis_index("sub")
    tile = lax.axis_index("tile")
    parity = lax.rem(me, 2)
    mate = me + 1 - 2 * parity
    pair = me // 2
    has_up = tile > 0
    has_down = tile < tiles - 1
    up, down = tile - 1, tile + 1
    windows, pieces = windows_of(rows), pieces_of(rows)
    groups = len(REACHES)

    tables = [
        pltpu.make_async_copy(depth_in, depth_tab, load_sem.at[2]),
        pltpu.make_async_copy(spread_in, spread_tab, load_sem.at[3]),
        pltpu.make_async_copy(mixing_in, mixing, load_sem.at[4]),
    ]
    own = pl.ds(HALO, rows)
    pltpu.make_async_copy(terrain, T, load_sem.at[0]).start()
    for copy in tables:
        copy.start()
    for b in range(blocks):
        at = pl.ds(b * LANES, LANES)
        pltpu.make_async_copy(
            states.at[0, :, :, at], S.at[pl.ds(0, 3), own, b % 2, b // 2], load_sem.at[1]
        ).start()

    barrier = pltpu.get_barrier_semaphore()
    pl.semaphore_signal(barrier, inc=1, device_id={"sub": mate})
    for k in range(1, pairs):
        pl.semaphore_signal(
            barrier, inc=1, device_id={"sub": lax.rem(pair + k, pairs) * 2 + parity}
        )

    @pl.when(has_up)
    def _():
        pl.semaphore_signal(barrier, inc=1, device_id={"tile": up})

    @pl.when(has_down)
    def _():
        pl.semaphore_signal(barrier, inc=1, device_id={"tile": down})

    @pl.when(jnp.logical_not(has_up))
    def _():
        S[:, 0:HALO] = jnp.zeros((5, HALO, 2, half, LANES), jnp.float32)

    @pl.when(jnp.logical_not(has_down))
    def _():
        S[:, HALO + rows:] = jnp.zeros((5, HALO, 2, half, LANES), jnp.float32)

    pltpu.make_async_copy(T, T, load_sem.at[0]).wait()
    for copy in tables:
        copy.wait()
    def lookup(i, carry):
        for j in range(SUBLANES):
            for e in range(2):
                first = (i * blocks + e) * SUBLANES + j
                kind = T[pl.ds(first, half, stride=2 * SUBLANES), :]
                depth = jnp.zeros(kind.shape, jnp.float32)
                kappa = jnp.zeros(kind.shape, jnp.float32)
                for n in range(nclass):
                    hit = kind == n
                    depth = jnp.where(hit, depth_tab[n], depth)
                    kappa = jnp.where(hit, spread_tab[n], kappa)
                S[DEPTH, HALO + i * SUBLANES + j, e] = depth
                S[KAPPA, HALO + i * SUBLANES + j, e] = kappa
        return carry

    lax.fori_loop(0, rows // SUBLANES, lookup, 0)
    loaded = S.at[pl.ds(0, 3), own]
    pltpu.make_async_copy(loaded, loaded, load_sem.at[1]).wait()

    def edge(way, near, far):
        count = far - near + 1
        if way == 0:
            return pl.ds(HALO + rows - far, count), pl.ds(HALO - far, count)
        return pl.ds(HALO + near - 1, count), pl.ds(HALO + rows + near - 1, count)

    def to_tile(way, source, target, send, recv):
        return pltpu.make_async_remote_copy(
            src_ref=source, dst_ref=target, send_sem=send, recv_sem=recv,
            device_id={"tile": down if way == 0 else up}, device_id_type=pl.DeviceIdType.MESH,
        )

    land_rows = ((DEPTH, HALO), (KAPPA, DSTEPS - 1))
    land_bytes = S.at[0, pl.ds(0, HALO + DSTEPS - 1), 0]

    def land_copies(way):
        copies = []
        for f, far in land_rows:
            source, target = edge(way, 1, far)
            copies.append(to_tile(
                way, S.at[f, source, parity], S.at[f, target, parity],
                tile_send.at[way], land_recv.at[way],
            ))
        return copies

    def pass_copies(way):
        copies = []
        for f, far in land_rows:
            _, at = edge(way, 1, far)
            copies.append(pltpu.make_async_remote_copy(
                src_ref=S.at[f, at, parity], dst_ref=S.at[f, at, parity],
                send_sem=tile_send.at[1 - way], recv_sem=pass_recv.at[way],
                device_id={"sub": mate}, device_id_type=pl.DeviceIdType.MESH,
            ))
        return copies

    def halo_copies(way, g):
        near, far = (REACHES[g - 1] if g > 0 else 0) + 1, REACHES[g]
        parts = [(pl.ds(0, 3), near, far)]
        if g == groups - 1:
            parts = [(pl.ds(0, 3), near, far - 1), (pl.ds(1, 1), far, far)]
        copies = []
        for fields, first, last in parts:
            source, target = edge(way, first, last)
            copies.append(to_tile(
                way, S.at[fields, source], S.at[fields, target],
                tile_send.at[way], halo_recv.at[way, g],
            ))
        return copies

    def halo_bytes(g):
        count = REACHES[g] - (REACHES[g - 1] if g > 0 else 0)
        return S.at[0, pl.ds(0, 3 * count - (2 if g == groups - 1 else 0))]

    def wait_for(some, sem):
        pltpu.make_async_copy(some, some, sem).wait()

    comes = (has_up, has_down)
    goes = (has_down, has_up)

    def enter():
        pl.semaphore_wait(
            barrier, pairs + has_up.astype(jnp.int32) + has_down.astype(jnp.int32)
        )
    def send_land():
        for way in range(2):

            @pl.when(goes[way])
            def _():
                for copy in land_copies(way):
                    copy.start()

    def send_halo(g):
        for way in range(2):

            @pl.when(goes[way])
            def _():
                for copy in halo_copies(way, g):
                    copy.start()

    def pass_land():
        for way in range(2):

            @pl.when(comes[way])
            def _():
                wait_for(land_bytes, land_recv.at[way])
                for copy in pass_copies(way):
                    copy.start()

    def take_land():
        for way in range(2):

            @pl.when(comes[way])
            def _():
                wait_for(land_bytes, pass_recv.at[way])

    def take_halo(g):
        for way in range(2):

            @pl.when(comes[way])
            def _():
                wait_for(halo_bytes(g), halo_recv.at[way, g])

    lane = lax.broadcasted_iota(jnp.int32, (1, half, LANES), 2)
    is_first, is_last = lane == 0, lane == LANES - 1

    def get(ref, lead, start, count):
        at = pl.ds(HALO + start, count)
        return ref[lead + (at, 0)], ref[lead + (at, 1)]

    def put(ref, lead, start, count, value):
        at = pl.ds(HALO + start, count)
        ref[lead + (at, 0)] = value[0]
        ref[lead + (at, 1)] = value[1]

    def each(function, *values):
        return tuple(function(*parts) for parts in zip(*values))

    def sides(value):
        even, odd = value
        even_up, odd_up = pltpu.roll(even, LANES - 1, 2), pltpu.roll(odd, LANES - 1, 2)
        even_down, odd_down = pltpu.roll(even, 1, 2), pltpu.roll(odd, 1, 2)
        following = (
            jnp.where(is_last, odd_up, even_up),
            jnp.where(is_last, pltpu.roll(even_up, half - 1, 1), odd_up),
        )
        previous = (
            jnp.where(is_first, pltpu.roll(odd_down, 1, 1), even_down),
            jnp.where(is_first, even_down, odd_down),
        )
        return following, previous

    def col_diff(value):
        following, previous = sides(value)
        return each(lambda a, b: a - b, following, previous)

    def row_diff(value):
        return each(lambda a: a[2:] - a[:-2], value)

    def inner_rows(value):
        return each(lambda a: a[1:-1], value)

    up_scale = jnp.where(has_up, 1.0, 0.0)
    down_scale = jnp.where(has_down, 1.0, 0.0)

    def masked(value, start, count):
        if not isinstance(start, int) or (start >= 0 and start + count <= rows):
            return value
        scales = []
        for r in range(start, start + count):
            scales.append(up_scale if r < 0 else down_scale if r >= rows else None)

        def scale(part):
            return jnp.concatenate(
                [part[i:i + 1] if s is None else part[i:i + 1] * s for i, s in enumerate(scales)], 0
            )

        return each(scale, value)

    def field(step, f):
        return (S, (f,)) if step == 0 else (E, (step - 1, f))

    def height_stage(step, start, count):
        h_ref, h_at = field(step, 0)
        u_ref, u_at = field(step, 1)
        v_ref, v_at = field(step, 2)
        wide_d = get(S, (DEPTH,), start - 1, count + 2)
        flux_x = each(jnp.multiply, wide_d, get(u_ref, u_at, start - 1, count + 2))
        flux_y = each(jnp.multiply, inner_rows(wide_d), get(v_ref, v_at, start, count))
        h = get(h_ref, h_at, start, count)
        new_h = each(
            lambda a, x, y: a - (time_step * 0.5) * (x + y), h, row_diff(flux_x), col_diff(flux_y)
        )
        put(E, (step, 0), start, count, masked(new_h, start, count))

    def wind_stage(step, start, count):
        u_ref, u_at = field(step, 1)
        v_ref, v_at = field(step, 2)
        wide_h = get(E, (step, 0), start - 1, count + 2)
        u = get(u_ref, u_at, start, count)
        v = get(v_ref, v_at, start, count)
        pull, turn = time_step * gravity * 0.5, time_step * coriolis
        new_u = each(lambda a, b, x: a - pull * x + turn * b, u, v, row_diff(wide_h))
        new_v = each(lambda a, b, y: b - pull * y - turn * a, u, v, col_diff(inner_rows(wide_h)))
        if step == FSTEPS - 1:
            new_u, new_v = masked(new_u, start, count), masked(new_v, start, count)
        put(E, (step, 1), start, count, new_u)
        put(E, (step, 2), start, count, new_v)

    def spread(ref, at, start, count, kappa, rest):
        wide = get(ref, at, start - 1, count + 2)
        w = inner_rows(wide)
        following, previous = sides(w)
        return each(
            lambda a, n, p, c, k, r: r * c + k * ((a[2:] + a[:-2]) + (n + p)),
            wide, following, previous, w, kappa, rest,
        )

    def coefficients(start, count):
        kappa = get(S, (KAPPA,), start, count)
        return kappa, each(lambda k: 1.0 - 4.0 * k, kappa)

    def spread_stage(step, start, count):
        kappa, rest = coefficients(start, count)
        for f in range(6):
            if step == 0:
                ref, at = field(FSTEPS, f - 3) if f >= 3 else field(0, f)
            else:
                ref, at = W, (step - 1, f)
            put(W, (step, f), start, count, spread(ref, at, start, count, kappa, rest))

    stages = []
    for step in range(FSTEPS):
        stages.append((functools.partial(height_stage, step), HALO - 1 - 2 * step, 16))
        stages.append((functools.partial(wind_stage, step), HALO - 2 - 2 * step, 16))
    for step in range(DSTEPS):
        stages.append((functools.partial(spread_stage, step), DSTEPS - 1 - step, 4))

    def advance(stage, lo, hi, size):
        count = hi - lo
        whole = count // size
        if whole > 1:

            def body(i, carry):
                stage(lo + i * size, size)
                return carry

            for i in range(whole):
                body(i, 0)
            lo += whole * size
        elif whole == 1:
            stage(lo, size)
            lo += size
        if hi > lo:
            stage(lo, hi - lo)

    def compute(g, chosen=stages):
        for stage, margin, size in chosen:
            for lo, count, _ in pieces[g]:
                hi = lo + count
                if g == 0:
                    advance(stage, lo - margin, hi + margin, size)
                elif hi <= windows[0][0]:
                    advance(stage, lo - margin, hi - margin, size)
                else:
                    advance(stage, lo + margin, hi + margin, size)

    moves, spreads = stages[:2 * FSTEPS], stages[2 * FSTEPS:]

    def spread_inner():
        lo, hi = windows[1]
        for stage, margin, size in spreads:
            advance(stage, lo - margin, hi + margin, size)

    later = jnp.minimum(me + 1, subs - 1)
    keep = jnp.where(me < subs - 1, 1.0, 0.0)

    def weights(s):
        return mixing[s, me], mixing[s, later] * keep

    dest_pair = [lax.rem(pair + k, pairs) for k in range(pairs)]
    w_mine = [weights(q * 2 + parity) for q in dest_pair]
    w_mate = [weights(q * 2 + 1 - parity) for q in dest_pair]
    order = list(range(1, pairs)) + [0]

    def span(g):
        first = pieces[g][0][2]
        return pl.ds(first, sum(count for _, count, _ in pieces[g]))

    def a_copy(g, k):
        at = (k, slice(None), span(g))
        return pltpu.make_async_remote_copy(
            src_ref=send_a.at[at], dst_ref=recv_a.at[at],
            send_sem=a_send, recv_sem=a_recv.at[g * (pairs - 1) + k if k > 0 else 0],
            device_id={"sub": mate}, device_id_type=pl.DeviceIdType.MESH,
        )

    def b_copy(g, k):
        at = (k - 1, slice(None), span(g))
        return pltpu.make_async_remote_copy(
            src_ref=send_b.at[at], dst_ref=recv_b.at[at],
            send_sem=b_send, recv_sem=b_recv.at[g, k - 1],
            device_id={"sub": dest_pair[k] * 2 + parity},
            device_id_type=pl.DeviceIdType.MESH,
        )

    def mix_first(weight, ref, k):
        (lo, count, place), = pieces[0]
        a, b = weight

        def mix(start, n):
            for f in range(3):
                ref_end, at_end = field(FSTEPS, f)
                ends = get(ref_end, at_end, start, n)
                put(Z, (0, f), start, n, each(lambda x, y: a * x - b * y, get(S, (f,), start, n), ends))

        def spread_mixed(step, start, n):
            kappa, rest = coefficients(start, n)
            for f in range(3):
                new = spread(Z, (step, f), start, n, kappa, rest)
                if step < DSTEPS - 1:
                    put(Z, (step + 1, f), start, n, new)
                else:
                    for e in range(2):
                        ref[k, f, pl.ds(place + start - lo, n), e] = new[e]

        advance(mix, lo - DSTEPS, lo + count + DSTEPS, 4)
        for step in range(DSTEPS):
            margin = DSTEPS - 1 - step
            advance(functools.partial(spread_mixed, step), lo - margin, lo + count + margin, 4)

    def mate_terms(g, k):
        for lo, count, place in pieces[g]:
            at = pl.ds(place, count)
            for f in range(3):
                start = W[DSTEPS - 1, f, pl.ds(HALO + lo, count)]
                end = W[DSTEPS - 1, 3 + f, pl.ds(HALO + lo, count)]
                a, b = w_mate[k]
                send_a[k, f, at] = a * start - b * end
        a_copy(g, k).start()

    def own_terms(g, k):
        for lo, count, place in pieces[g]:
            at = pl.ds(place, count)
            for f in range(3):
                start = W[DSTEPS - 1, f, pl.ds(HALO + lo, count)]
                end = W[DSTEPS - 1, 3 + f, pl.ds(HALO + lo, count)]
                a, b = w_mine[k]
                mine = a * start - b * end
                if k == 0:
                    M[f, at] = mine
                else:
                    send_b[k - 1, f, at] = mine

    def terms(g):
        for k in order:
            mate_terms(g, k)
        for k in order:
            own_terms(g, k)

    def join(g):
        for k in range(1, pairs):
            a_copy(g, k).wait_recv()
            at = (k - 1, slice(None), span(g))
            send_b[at] = send_b[at] + recv_a[(k, slice(None), span(g))]
            b_copy(g, k).start()

    def finish(g):
        for k in range(1, pairs):
            b_copy(g, k).wait_recv()
        for lo, count, place in pieces[g]:
            for f in range(3):
                for i in range(count):
                    r = lo + i
                    total = M[f, place + i] + recv_a[0, f, place + i]
                    for k in range(1, pairs):
                        total = total + recv_b[k - 1, f, place + i]
                    base = (f * (rows // SUBLANES) + r // SUBLANES) * blocks * SUBLANES + r % SUBLANES
                    for e in range(2):
                        out[pl.ds(base + e * SUBLANES, half, stride=2 * SUBLANES), :] = total[e]

    enter()
    send_land()
    send_halo(0)
    if pairs == 2:
        compute(0, moves)
        mix_first(w_mate[1], send_a, 1)
        a_copy(0, 1).start()
        send_halo(1)
        mix_first(w_mine[1], send_b, 0)
        join(0)
        compute(1, moves)
        spread_inner()
        terms(1)
    else:
        compute(0)
        terms(0)
        join(0)
        send_halo(1)
        compute(1)
        terms(1)
    pass_land()
    for g in range(2, groups):
        send_halo(g)
    join(1)
    if pairs == 2:
        mate_terms(0, 0)
        own_terms(0, 0)
    take_land()
    for g in range(groups):
        take_halo(g)
        compute(g + 2)
        terms(g + 2)
        join(g + 2)
    wait_for(recv_a.at[0], a_recv.at[0])
    for g in range(groups + 2):
        finish(g)

    pltpu.make_async_copy(send_a, send_a, a_send).wait()
    if pairs > 1:
        pltpu.make_async_copy(send_b, send_b, b_send).wait()
    sent = S.at[0, pl.ds(0, 3 * HALO - 2 + HALO + DSTEPS - 1)]
    for way in range(2):

        @pl.when(goes[way])
        def _():
            wait_for(sent, tile_send.at[way])


def solution(mesh):
    subs, tiles = mesh.shape["sub"], mesh.shape["tile"]

    def local(states, terrain, depth_table, spread_table, mixing):
        _, fields, rows, cols = states.shape
        pairs = subs // 2
        many = max(pairs - 1, 1)
        blocks = cols // LANES
        row = (2, blocks // 2, LANES)
        tall = rows + 2 * HALO
        dma = pltpu.SemaphoreType.DMA
        phases = len(windows_of(rows))
        vmem = pltpu.VMEM

        def flat(value):
            tiles_last = value.reshape(rows // SUBLANES, SUBLANES, blocks, LANES)
            return tiles_last.transpose(0, 2, 1, 3).reshape(-1, LANES)

        result = pl.pallas_call(
            functools.partial(kernel, subs, tiles, rows, cols, depth_table.shape[0]),
            out_shape=jax.ShapeDtypeStruct((fields * rows * blocks, LANES), jnp.float32),
            in_specs=[pl.BlockSpec(memory_space=pltpu.HBM)] * 5,
            out_specs=pl.BlockSpec(memory_space=pltpu.VMEM),
            scratch_shapes=[
                pltpu.SMEM(depth_table.shape, jnp.float32),
                pltpu.SMEM(spread_table.shape, jnp.float32),
                pltpu.SMEM(mixing.shape, jnp.float32),
                vmem((rows * blocks, LANES), jnp.int32),
                vmem((5, tall) + row, jnp.float32),
                vmem((FSTEPS, fields, tall) + row, jnp.float32),
                vmem((DSTEPS, 2 * fields, tall) + row, jnp.float32),
                vmem((DSTEPS, fields, tall) + row, jnp.float32),
                vmem((pairs, fields, rows) + row, jnp.float32),
                vmem((pairs, fields, rows) + row, jnp.float32),
                vmem((many, fields, rows) + row, jnp.float32),
                vmem((many, fields, rows) + row, jnp.float32),
                vmem((fields, rows) + row, jnp.float32),
                dma((5,)),
                dma((2,)),
                dma((2,)),
                dma((2,)),
                dma((2, len(REACHES))),
                dma(()),
                dma((phases * (pairs - 1) + 1,)),
                dma(()),
                dma((phases, many)),
            ],
            compiler_params=pltpu.CompilerParams(
                collective_id=0, has_side_effects=True, vmem_limit_bytes=46 * 1024 * 1024
            ),
            name="gradient",
        )(
            *(
                pltpu.with_memory_space_constraint(value, pltpu.HBM)
                for value in (depth_table, spread_table, mixing, states, flat(terrain))
            )
        )
        tiled = result.reshape(fields, rows // SUBLANES, blocks, SUBLANES, LANES)
        return tiled.transpose(0, 1, 3, 2, 4).reshape(states.shape)

    in_specs = (P("sub", None, "tile", None), P("tile", None), P(), P(), P())
    out_specs = P("sub", None, "tile", None)
    return jax.shard_map(local, mesh=mesh, in_specs=in_specs, out_specs=out_specs, check_vma=False)
```
